128 devices in a mesh: layer: 32 (over y, x, core), dp: 4 (over z).
Axes of the slice: x: 4, y: 4, z: 4, core: 2. Of those that a mesh axis runs over, the one named last changes fastest.
Arguments:
- inputs: float32 [512, 1024], P('dp'), may hold values from -6 to 6
- guesses: float32 [32, 512, 1024], P('layer', 'dp'), may hold values from -6 to 6
- weights: bfloat16 [128, 1024, 1024], P('layer'), may hold values from -0.1875 to 0.1875
- biases: float32 [128, 1024], P('layer'), may hold values from -3 to 3
- adjoint: bfloat16 [32, 512, 1024], P('layer', 'dp'), may hold values from -6 to 6
Outputs:
- new_states: float32 [32, 512, 1024], P('layer', 'dp')
- coarse_states: float32 [32, 512, 1024], P('layer', 'dp')
- weight_grad: float32 [32, 1024, 1024], P('layer', None, 'dp')
The draws below stay inside these ranges and needn't reach their ends.
All inputs are finite; a program needn't handle non-finite values.
Results may differ from the reference program's by a relative error of at most 0.007.
Values may be sent and summed in bfloat16 or wider, within the bound.
A program may use at most 64 MiB of HBM per device.

```python
import jax
import jax.numpy as jnp
from jax import lax

D = 1024
ROWS = 512
POINTS = 32
LAYERS = 128


def levels(key, shape, split, least, high):
    level, own = 1.0, jax.random.fold_in(key, 6)
    for axis_at, shards_of in split:
        draws = jnp.exp(jax.random.uniform(jax.random.fold_in(own, axis_at), (shards_of,), jnp.float32, least / len(split), high / len(split)))
        level = level * jnp.repeat(draws, shape[axis_at] // shards_of).reshape([-1 if axis == axis_at else 1 for axis in range(len(shape))])
    return level


def bell_draw(rng, dims, scale, limit, shards=(), held_as=jnp.bfloat16):
    factor_of = levels(rng, dims, shards, -0.22, 0.18) if shards else 1.0
    drawn = jax.random.normal(rng, dims, jnp.float32) * scale * factor_of
    return jnp.minimum(jnp.maximum(drawn, -limit), limit).astype(held_as)


def setup_inputs(seed: int = 0) -> dict:
    key_of = jax.random.split(jax.random.key(seed), 6)
    return {
        "inputs": bell_draw(key_of[0], (ROWS, D), 1.0, 6.0, ((0, 4),), jnp.float32),
        "guesses": bell_draw(key_of[1], (POINTS, ROWS, D), 1.0, 6.0, ((0, 32), (1, 4)), jnp.float32),
        "weights": bell_draw(key_of[2], (LAYERS, D, D), D ** -0.5, 0.1875, ((0, 32),)),
        "biases": bell_draw(key_of[3], (LAYERS, D), 0.5, 3.0, ((0, 32),), jnp.float32),
        "adjoint": bell_draw(key_of[4], (POINTS, ROWS, D), 1.0, 6.0, ((0, 32), (1, 4))),
    }


def matmul_all(states, weight_stack):
    return jnp.einsum('prd,pde->pre', states.astype(jnp.bfloat16).astype(jnp.float32), weight_stack.astype(jnp.float32))


def advance_all(states, weight_stack, bias_stack, step_size):
    pre_tanh = matmul_all(states, weight_stack) + bias_stack[:, None, :]
    return states + step_size * jnp.tanh(pre_tanh), pre_tanh


def previous(inputs, states):
    return jnp.concatenate([inputs[None], states[:-1]], axis=0)


def fine_all(starts, weights, biases, step_size):
    current = starts
    last_in = starts
    pre_tanh = starts
    for layer_idx in range(4):
        if layer_idx == 3:
            last_in = current
        current, pre_tanh = advance_all(current, weights[layer_idx::4], biases[layer_idx::4], step_size)
    return current, last_in, pre_tanh


def reference(inputs, guesses, weights, biases, adjoint):
    step_size = 4.0 / LAYERS
    coarse_w = weights[0::4]
    coarse_b = biases[0::4]
    groups = POINTS // 4
    relaxed = fine_all(previous(inputs, guesses), weights, biases, step_size)[0]
    relaxed_prev = previous(inputs, relaxed)
    ahead = fine_all(relaxed_prev, weights, biases, step_size)[0]
    forcing = ahead - advance_all(relaxed_prev, coarse_w, coarse_b, 4.0 * step_size)[0]
    group_w = coarse_w.reshape(groups, 4, D, D)
    group_b = coarse_b.reshape(groups, 4, D)
    group_f = forcing.reshape(groups, 4, ROWS, D)
    values = relaxed.reshape(groups, 4, ROWS, D)

    def level_step(states, slot):
        return advance_all(states, group_w[:, slot], group_b[:, slot], 4.0 * step_size)[0] + group_f[:, slot]

    def c_prev(values):
        return jnp.concatenate([inputs[None], values[:-1, 3]], axis=0)

    def f_relax(values):
        start = c_prev(values)
        for slot in range(3):
            start = level_step(start, slot)
            values = values.at[:, slot].set(start)
        return values

    values = f_relax(values)
    values = values.at[:, 3].set(level_step(values[:, 2], 3))
    values = f_relax(values)
    flat = values.reshape(POINTS, ROWS, D)
    update = advance_all(previous(inputs, flat), coarse_w, coarse_b, 4.0 * step_size)[0] + forcing
    start_block = jnp.broadcast_to(inputs[None], (4, ROWS, D))
    below = jnp.concatenate([start_block, flat[:-4]], axis=0)
    coarse_force = update - advance_all(below, coarse_w, coarse_b, 16.0 * step_size)[0]

    def chain_step(carry, pieces):
        weight, bias_row, force = pieces
        result = advance_all(carry, weight, bias_row, 16.0 * step_size)[0] + force
        return result, result

    _, solved = lax.scan(chain_step, start_block, (group_w, group_b, coarse_force.reshape(groups, 4, ROWS, D)))
    values = values.at[:, 3].set(solved[:, 3])
    coarse_states = solved.reshape(POINTS, ROWS, D) - relaxed
    values = f_relax(values)
    corrected = values.reshape(POINTS, ROWS, D)
    new_states, last_in, pre_tanh = fine_all(previous(inputs, corrected), weights, biases, step_size)
    tanh_val = jnp.tanh(pre_tanh)
    deltas = (adjoint.astype(jnp.float32) * step_size * (1.0 - tanh_val * tanh_val)).astype(jnp.bfloat16)
    weight_grad = jnp.einsum('prd,pre->pde', last_in.astype(jnp.bfloat16).astype(jnp.float32), deltas.astype(jnp.float32))
    return new_states, coarse_states, weight_grad
```

```python
import functools

import jax
import jax.numpy as jnp
from jax import lax
from jax.experimental import pallas as pl
from jax.experimental.pallas import tpu as pltpu
from jax.sharding import PartitionSpec as P

MESH = pl.DeviceIdType.MESH
F32, BF16 = jnp.float32, jnp.bfloat16
CHUNK = 16
HALF = 64


def kernel(
    blocks,
    inputs,
    guesses,
    weights,
    biases,
    adjoint,
    new_out,
    coarse_out,
    grad_out,
    w_v,
    state,
    guess_in,
    relaxed,
    relaxed_in,
    forcing,
    first_v,
    update,
    level_in,
    below_in,
    below_step,
    solved,
    solved_in,
    final_v,
    final_in,
    early_send,
    early_in,
    a_all,
    d_send,
    d_all,
    w_sem,
    half_send,
    half_recv,
    level_send,
    level_recv,
    below_send,
    below_recv,
    solved_send,
    solved_recv,
    final_send,
    final_recv,
    early_sem,
    a_send,
    a_recv,
    d_ssem,
    d_rsem,
):
    rows = inputs.shape[0]
    chunks, halves = rows // CHUNK, rows // HALF
    h = 4.0 / (4 * blocks)
    me, zed = lax.axis_index("layer"), lax.axis_index("dp")
    planes = a_all.shape[0]
    pos = lax.rem(me + 1, 4)
    is_first, is_last = me == 0, me == blocks - 1
    is_c = pos == 0

    for layer in range(4):
        pltpu.make_async_copy(weights.at[layer], w_v.at[layer], w_sem.at[layer]).start()

    right, left = lax.rem(zed + 1, planes), lax.rem(zed + planes - 1, planes)
    across = lax.rem(zed + 2, planes)
    barrier = pltpu.get_barrier_semaphore()
    for step in (1, blocks - 1, 4, blocks - 4):
        pl.semaphore_signal(
            barrier, inc=1, device_id=(lax.rem(me + step, blocks), zed), device_id_type=MESH
        )
    for other in (right, left, across):
        pl.semaphore_signal(barrier, inc=1, device_id=(me, other), device_id_type=MESH)
    pl.semaphore_wait(barrier, 7)

    def hop(src, dst, send_sem, recv_sem, by):
        return pltpu.make_async_remote_copy(
            src_ref=src,
            dst_ref=dst,
            send_sem=send_sem,
            recv_sem=recv_sem,
            device_id=(lax.rem(me + by, blocks), zed),
            device_id_type=MESH,
        )

    def zhop(src, dst, send_sem, recv_sem, to):
        return pltpu.make_async_remote_copy(
            src_ref=src,
            dst_ref=dst,
            send_sem=send_sem,
            recv_sem=recv_sem,
            device_id=(me, to),
            device_id_type=MESH,
        )

    def chunk_rows(c):
        return pl.ds(pl.multiple_of(c * CHUNK, CHUNK), CHUNK)

    def half_rows(c):
        return pl.ds(pl.multiple_of(c * HALF, HALF), HALF)

    def act(x, layer):
        z = jnp.dot(x.astype(BF16), w_v[layer], preferred_element_type=F32) + biases[layer]
        return jnp.tanh(z)

    def each(count, body):
        def step(c, carry):
            body(c)
            return carry

        lax.fori_loop(0, count, step, 0)

    def guess_hop(c):
        r = half_rows(c)
        return hop(guesses.at[0, r], guess_in.at[r], half_send.at[0, c], half_recv.at[0, c], 1)

    @pl.when(jnp.logical_not(is_last))
    def _():
        each(halves, lambda c: guess_hop(c).start())

    @pl.when(is_first)
    def _():
        guess_in[...] = inputs[...]
        relaxed_in[...] = inputs[...]

    for layer in range(4):
        pltpu.make_async_copy(weights.at[layer], w_v.at[layer], w_sem.at[layer]).wait()

    def relaxed_hop(c):
        r = half_rows(c)
        return hop(relaxed.at[r], relaxed_in.at[r], half_send.at[1, c], half_recv.at[1, c], 1)

    def relax_half(c):
        r = half_rows(c)

        @pl.when(jnp.logical_not(is_first))
        def _():
            guess_hop(c).wait_recv()

        relaxed[r, :] = guess_in[r, :]

        def layer_step(layer, carry):
            u = relaxed[r, :]
            relaxed[r, :] = u + h * act(u, layer)
            return carry

        lax.fori_loop(0, 4, layer_step, 0)

        @pl.when(jnp.logical_not(is_last))
        def _():
            relaxed_hop(c).start()

    each(halves, relax_half)

    def forcing_half(c):
        r = half_rows(c)

        @pl.when(jnp.logical_not(is_first))
        def _():
            relaxed_hop(c).wait_recv()

        u = relaxed_in[r, :]
        t = act(u, 0)
        coarse = u + (4.0 * h) * t
        first_v[r, :] = coarse
        state[r, :] = u + h * t

        def layer_step(layer, carry):
            u = state[r, :]
            state[r, :] = u + h * act(u, layer)
            return carry

        lax.fori_loop(1, 4, layer_step, 0)
        force = state[r, :] - first_v[r, :]
        forcing[r, :] = force
        first_v[r, :] = first_v[r, :] + force

    each(halves, forcing_half)

    slot = jnp.where(is_c, 1, 0)

    def level_hop(sweep, c, src):
        r = chunk_rows(c)
        return hop(
            src.at[r], level_in.at[sweep, r], level_send.at[sweep, c], level_recv.at[sweep, c], 1
        )

    def first_hop(c):
        r = chunk_rows(c)
        return hop(
            first_v.at[r], level_in.at[slot, r], level_send.at[0, c], level_recv.at[slot, c], 1
        )

    def below_hop(c):
        r = chunk_rows(c)
        return hop(first_v.at[r], below_in.at[r], below_send.at[c], below_recv.at[c], 4)

    def first_sweep(c):
        r = chunk_rows(c)

        @pl.when(pos != 1)
        def _():
            level_hop(0, c, first_v).wait_recv()
            u = level_in[0, r, :]
            first_v[r, :] = u + (4.0 * h) * act(u, 0) + forcing[r, :]

        @pl.when(jnp.logical_not(is_last))
        def _():
            first_hop(c).start()

        @pl.when(jnp.logical_and(is_c, jnp.logical_not(is_last)))
        def _():
            below_hop(c).start()

    each(chunks, first_sweep)

    @pl.when(is_c)
    def _():
        def below_chunk(c):
            r = chunk_rows(c)

            @pl.when(me >= 4)
            def _():
                below_hop(c).wait_recv()

            @pl.when(me < 4)
            def _():
                below_in[r, :] = inputs[r, :]

            u = below_in[r, :]
            below_step[r, :] = u + (16.0 * h) * act(u, 0)

        each(chunks, below_chunk)

    @pl.when(is_first)
    def _():
        level_in[1] = inputs[...]

    def second_sweep(c):
        r = chunk_rows(c)

        @pl.when(jnp.logical_not(is_first))
        def _():
            level_hop(1, c, update).wait_recv()

        u = level_in[1, r, :]
        update[r, :] = u + (4.0 * h) * act(u, 0) + forcing[r, :]

        @pl.when(jnp.logical_not(is_c))
        def _():
            level_hop(1, c, update).start()

    each(chunks, second_sweep)

    def early_hop():
        return hop(early_send, early_in, early_sem.at[0], early_sem.at[1], 4)

    @pl.when(jnp.logical_not(is_c))
    def _():
        early_send[...] = update[...].astype(BF16)

        @pl.when(me < blocks - 4)
        def _():
            early_hop().start()

        @pl.when(me >= 4)
        def _():
            early_hop().wait_recv()

        @pl.when(me < 4)
        def _():
            early_in[...] = inputs[...].astype(BF16)

        below_step[...] = early_in[...].astype(F32) + (16.0 * h) * act(early_in[...], 0)
        step_two = below_step[...]
        coarse_out[0] = step_two + (update[...] - step_two) - relaxed[...]

    def solved_hop(c):
        r = chunk_rows(c)
        return hop(solved.at[r], solved_in.at[r], solved_send.at[c], solved_recv.at[c], 4)

    def final_hop(c, src):
        r = chunk_rows(c)
        return hop(src.at[r], final_in.at[r], final_send.at[c], final_recv.at[c], 1)

    @pl.when(is_c)
    def _():
        def solve_chunk(c):
            r = chunk_rows(c)
            force = update[r, :] - below_step[r, :]

            @pl.when(me >= 4)
            def _():
                solved_hop(c).wait_recv()
                u = solved_in[r, :]
                solved[r, :] = u + (16.0 * h) * act(u, 0) + force

            @pl.when(me < 4)
            def _():
                solved[r, :] = below_step[r, :] + force

            @pl.when(jnp.logical_not(is_last))
            def _():
                solved_hop(c).start()
                final_hop(c, solved).start()

            coarse_out[0, r, :] = solved[r, :] - relaxed[r, :]

        each(chunks, solve_chunk)

    @pl.when(is_first)
    def _():
        final_in[...] = inputs[...]

    def final_sweep(c):
        r = chunk_rows(c)

        @pl.when(jnp.logical_not(is_first))
        def _():
            final_hop(c, final_v).wait_recv()

        u = final_in[r, :]
        t = act(u, 0)
        final_v[r, :] = u + (4.0 * h) * t + forcing[r, :]

        @pl.when(jnp.logical_not(is_c))
        def _():
            final_hop(c, final_v).start()

        state[r, :] = u + h * t

    each(chunks, final_sweep)

    def a_hop(side, c):
        r = half_rows(c)
        return zhop(
            a_all.at[zed, r],
            a_all.at[zed, r],
            a_send.at[side, c],
            a_recv.at[side, c],
            right if side == 0 else left,
        )

    def a_came(side, c):
        r = half_rows(c)
        source = left if side == 0 else right
        return zhop(
            a_all.at[source, r],
            a_all.at[source, r],
            a_send.at[side, c],
            a_recv.at[side, c],
            right if side == 0 else left,
        )

    def a_relay(side):
        r = half_rows(side)
        source = left if side == 0 else right
        return zhop(
            a_all.at[source, r],
            a_all.at[source, r],
            a_send.at[2, side],
            a_recv.at[2, side],
            right if side == 0 else left,
        )

    def a_relayed(side):
        r = half_rows(side)
        return zhop(
            a_all.at[across, r],
            a_all.at[across, r],
            a_send.at[2, side],
            a_recv.at[2, side],
            right if side == 0 else left,
        )

    def d_hop(j, c):
        r = half_rows(c)
        to = lax.rem(zed + j, planes)
        return zhop(
            d_send.at[to, r], d_all.at[zed, r], d_ssem.at[j - 1, c], d_rsem.at[j - 1, c], to
        )

    def d_came(j, c):
        r = half_rows(c)
        source = lax.rem(zed + planes - j, planes)
        return zhop(
            d_send.at[zed, r], d_all.at[source, r], d_ssem.at[j - 1, c], d_rsem.at[j - 1, c], source
        )

    cols = grad_out.shape[2]

    def block_half(c):
        r = half_rows(c)

        def layer_step(layer, carry):
            u = state[r, :]
            state[r, :] = u + h * act(u, layer)
            return carry

        lax.fori_loop(1, 3, layer_step, 0)
        u = state[r, :]
        x = u.astype(BF16)
        a_all[zed, r, :] = x
        a_hop(0, c).start()
        a_hop(1, c).start()
        t = act(x, 3)
        new_out[0, r, :] = u + h * t
        delta = (adjoint[0, r, :].astype(F32) * h * (1.0 - t * t)).astype(BF16)
        for j in range(planes):
            d_send[j, r, :] = delta[:, j * cols : (j + 1) * cols]
        d_all[zed, r, :] = d_send[zed, r, :]
        for j in range(1, planes):
            d_hop(j, c).start()

    each(halves, block_half)

    for side in range(2):
        a_came(side, side).wait_recv()
        a_relay(side).start()
    for side in range(2):
        a_came(side, 1 - side).wait_recv()
    for j in range(1, planes):
        for c in range(halves):
            d_came(j, c).wait_recv()
    for side in range(2):
        a_relayed(side).wait_recv()
    grad_out[0] = lax.dot_general(
        a_all[...].reshape(planes * rows, a_all.shape[2]),
        d_all[...].reshape(planes * rows, cols),
        (((0,), (0,)), ((), ())),
        preferred_element_type=F32,
    )

    @pl.when(jnp.logical_not(is_last))
    def _():
        def sent(c):
            guess_hop(c).wait_send()
            relaxed_hop(c).wait_send()

        each(halves, sent)

        def sent_chunk(c):
            first_hop(c).wait_send()
            final_hop(c, final_v).wait_send()

        each(chunks, sent_chunk)

    @pl.when(jnp.logical_not(is_c))
    def _():
        each(chunks, lambda c: level_hop(1, c, update).wait_send())

        @pl.when(me < blocks - 4)
        def _():
            early_hop().wait_send()

    @pl.when(jnp.logical_and(is_c, jnp.logical_not(is_last)))
    def _():
        def sent_c(c):
            below_hop(c).wait_send()
            solved_hop(c).wait_send()

        each(chunks, sent_c)

    for side in range(2):
        for c in range(halves):
            a_hop(side, c).wait_send()
        a_relay(side).wait_send()
    for j in range(1, planes):
        for c in range(halves):
            d_hop(j, c).wait_send()


def solution(mesh):
    blocks, planes = mesh.shape["layer"], mesh.shape["dp"]

    def body(inputs, guesses, weights, biases, adjoint):
        rows, width = inputs.shape
        cols = width // planes
        chunks, halves = rows // CHUNK, rows // HALF
        whole = pltpu.VMEM((rows, width), F32)
        dma = pltpu.SemaphoreType.DMA
        vmem = pl.BlockSpec(memory_space=pltpu.VMEM)
        return pl.pallas_call(
            functools.partial(kernel, blocks),
            out_shape=(
                jax.ShapeDtypeStruct((1, rows, width), F32),
                jax.ShapeDtypeStruct((1, rows, width), F32),
                jax.ShapeDtypeStruct((1, width, cols), F32),
            ),
            in_specs=[vmem, vmem, pl.BlockSpec(memory_space=pl.ANY), vmem, vmem],
            out_specs=(vmem, vmem, vmem),
            scratch_shapes=[
                pltpu.VMEM((4, width, width), BF16),
                whole,
                whole,
                whole,
                whole,
                whole,
                whole,
                whole,
                pltpu.VMEM((2, rows, width), F32),
                whole,
                whole,
                whole,
                whole,
                whole,
                whole,
                pltpu.VMEM((rows, width), BF16),
                pltpu.VMEM((rows, width), BF16),
                pltpu.VMEM((planes, rows, width), BF16),
                pltpu.VMEM((planes, rows, cols), BF16),
                pltpu.VMEM((planes, rows, cols), BF16),
                dma((4,)),
                dma((2, halves)),
                dma((2, halves)),
                dma((2, chunks)),
                dma((2, chunks)),
                dma((chunks,)),
                dma((chunks,)),
                dma((chunks,)),
                dma((chunks,)),
                dma((chunks,)),
                dma((chunks,)),
                dma((2,)),
                dma((3, halves)),
                dma((3, halves)),
                dma((planes - 1, halves)),
                dma((planes - 1, halves)),
            ],
            compiler_params=pltpu.CompilerParams(
                collective_id=0, has_side_effects=True, vmem_limit_bytes=60 * 1024 * 1024
            ),
            name="mgrit_cycle",
        )(inputs, guesses, weights, biases.reshape(4, 1, width), adjoint)

    return jax.shard_map(
        body,
        mesh=mesh,
        in_specs=(
            P("dp", None),
            P("layer", "dp", None),
            P("layer", None, None),
            P("layer", None),
            P("layer", "dp", None),
        ),
        out_specs=(P("layer", "dp", None), P("layer", "dp", None), P("layer", None, "dp")),
        check_vma=False,
    )
```

```python
import functools

import jax
import jax.numpy as jnp
from jax import lax
from jax.experimental import pallas as pl
from jax.experimental.pallas import tpu as pltpu
from jax.sharding import PartitionSpec as P

MESH = pl.DeviceIdType.MESH
F32, BF16 = jnp.float32, jnp.bfloat16
CHUNK = 16
HALF = 64
PIECES = 8


def kernel(
    blocks,
    inputs,
    guesses,
    weights,
    biases,
    adjoint,
    new_out,
    coarse_out,
    grad_out,
    w_v,
    state,
    guess_in,
    relaxed,
    relaxed_in,
    forcing,
    first_v,
    update,
    level_in,
    below_in,
    below_step,
    own_step,
    solved,
    solved_a,
    solved_in,
    solved_back,
    final_v,
    final_in,
    v_mid,
    v_in,
    u_mid,
    u_in,
    w_mid,
    w_pair,
    b_send,
    b_pair,
    early_send,
    early_in,
    a_all,
    d_send,
    d_all,
    w_sem,
    half_send,
    half_recv,
    level_send,
    level_recv,
    below_send,
    below_recv,
    solved_send,
    solved_recv,
    final_send,
    final_recv,
    back_send,
    back_recv,
    mid_send,
    mid_recv,
    far_send,
    far_recv,
    wmid_send,
    wmid_recv,
    wfar_send,
    wfar_recv,
    b_sem,
    early_sem,
    a_send,
    a_recv,
    d_ssem,
    d_rsem,
):
    rows = inputs.shape[0]
    chunks, halves = rows // CHUNK, rows // HALF
    h = 4.0 / (4 * blocks)
    me, zed = lax.axis_index("layer"), lax.axis_index("dp")
    planes = a_all.shape[0]
    pos = lax.rem(me + 1, 4)
    is_first, is_last = me == 0, me == blocks - 1
    is_c = pos == 0
    seat, row = lax.rem(me, 8), me // 8
    is_a, is_pair, is_relay = seat == 3, seat == 7, seat == 1
    last_row = blocks // 8 - 1

    for layer in range(4):
        pltpu.make_async_copy(weights.at[layer], w_v.at[layer], w_sem.at[layer]).start()

    right, left = lax.rem(zed + 1, planes), lax.rem(zed + planes - 1, planes)
    across = lax.rem(zed + 2, planes)
    barrier = pltpu.get_barrier_semaphore()
    near = (1, 2, 3, 4, 6, 8)
    for step in near + tuple(blocks - step for step in near):
        pl.semaphore_signal(
            barrier, inc=1, device_id=(lax.rem(me + step, blocks), zed), device_id_type=MESH
        )
    for other in (right, left, across):
        pl.semaphore_signal(barrier, inc=1, device_id=(me, other), device_id_type=MESH)
    pl.semaphore_wait(barrier, 2 * len(near) + 3)

    def hop(src, dst, send_sem, recv_sem, by):
        return pltpu.make_async_remote_copy(
            src_ref=src,
            dst_ref=dst,
            send_sem=send_sem,
            recv_sem=recv_sem,
            device_id=(lax.rem(me + by + blocks, blocks), zed),
            device_id_type=MESH,
        )

    def zhop(src, dst, send_sem, recv_sem, to):
        return pltpu.make_async_remote_copy(
            src_ref=src,
            dst_ref=dst,
            send_sem=send_sem,
            recv_sem=recv_sem,
            device_id=(me, to),
            device_id_type=MESH,
        )

    def chunk_rows(c):
        return pl.ds(pl.multiple_of(c * CHUNK, CHUNK), CHUNK)

    def half_rows(c):
        return pl.ds(pl.multiple_of(c * HALF, HALF), HALF)

    def act(x, layer):
        z = jnp.dot(x.astype(BF16), w_v[layer], preferred_element_type=F32)
        return jnp.tanh(z + biases[pl.ds(layer, 1), :])

    def act_pair(x):
        z = jnp.dot(x.astype(BF16), w_pair[...], preferred_element_type=F32)
        return jnp.tanh(z + b_pair[0:1, :])

    def each(count, body):
        def step(c, carry):
            body(c)
            return carry

        lax.fori_loop(0, count, step, 0)

    def guess_hop(c):
        r = half_rows(c)
        return hop(guesses.at[0, r], guess_in.at[r], half_send.at[0, c], half_recv.at[0, c], 1)

    @pl.when(jnp.logical_not(is_last))
    def _():
        each(halves, lambda c: guess_hop(c).start())

    @pl.when(is_first)
    def _():
        guess_in[...] = inputs[...]
        relaxed_in[...] = inputs[...]

    def piece_rows(i):
        depth = weights.shape[1] // PIECES
        return pl.ds(pl.multiple_of(i * depth, depth), depth)

    def weight_mid(i):
        r = piece_rows(i)
        return hop(weights.at[0, r], w_mid.at[r], wmid_send.at[i], wmid_recv.at[i], -2)

    def weight_far(i):
        r = piece_rows(i)
        return hop(w_mid.at[r], w_pair.at[r], wfar_send.at[i], wfar_recv.at[i], 6)

    def bias_hop():
        return hop(b_send, b_pair, b_sem.at[0], b_sem.at[1], 4)

    @pl.when(is_a)
    def _():
        each(PIECES, lambda i: weight_mid(i).start())
        b_send[...] = jnp.broadcast_to(biases[0:1, :], b_send.shape)
        bias_hop().start()

    def relay_weights(start, stop):
        @pl.when(is_relay)
        def _():
            def forward(i):
                weight_mid(start + i).wait_recv()
                weight_far(start + i).start()

            each(stop - start, forward)

    def relaxed_hop(c):
        r = half_rows(c)
        return hop(relaxed.at[r], relaxed_in.at[r], half_send.at[1, c], half_recv.at[1, c], 1)

    def relax_half(c):
        r = half_rows(c)

        @pl.when(jnp.logical_not(is_first))
        def _():
            guess_hop(c).wait_recv()

        relaxed[r, :] = guess_in[r, :]

        def layer_step(layer, carry):
            @pl.when(c == 0)
            def _():
                pltpu.make_async_copy(weights.at[layer], w_v.at[layer], w_sem.at[layer]).wait()

            u = relaxed[r, :]
            relaxed[r, :] = u + h * act(u, layer)
            return carry

        lax.fori_loop(0, 4, layer_step, 0)

        @pl.when(jnp.logical_not(is_last))
        def _():
            relaxed_hop(c).start()

    each(halves, relax_half)
    relay_weights(0, 2)

    def forcing_half(c):
        r = half_rows(c)

        @pl.when(jnp.logical_not(is_first))
        def _():
            relaxed_hop(c).wait_recv()

        u = relaxed_in[r, :]
        t = act(u, 0)
        coarse = u + (4.0 * h) * t
        first_v[r, :] = coarse
        state[r, :] = u + h * t

        def layer_step(layer, carry):
            u = state[r, :]
            state[r, :] = u + h * act(u, layer)
            return carry

        lax.fori_loop(1, 4, layer_step, 0)
        force = state[r, :] - first_v[r, :]
        forcing[r, :] = force
        first_v[r, :] = first_v[r, :] + force

    each(halves, forcing_half)
    relay_weights(2, 5)

    slot = jnp.where(is_c, 1, 0)

    def level_hop(sweep, c, src):
        r = chunk_rows(c)
        return hop(
            src.at[r], level_in.at[sweep, r], level_send.at[sweep, c], level_recv.at[sweep, c], 1
        )

    def first_hop(c):
        r = chunk_rows(c)
        return hop(
            first_v.at[r], level_in.at[slot, r], level_send.at[0, c], level_recv.at[slot, c], 1
        )

    def below_hop(c):
        r = chunk_rows(c)
        return hop(first_v.at[r], below_in.at[r], below_send.at[c], below_recv.at[c], 8)

    def mid_hop(kind, c, src):
        r = chunk_rows(c)
        dst = (v_mid, u_mid)[kind]
        return hop(src.at[r], dst.at[r], mid_send.at[kind, c], mid_recv.at[kind, c], -2)

    def far_hop(kind, c):
        r = chunk_rows(c)
        src, dst = ((v_mid, v_in), (u_mid, u_in))[kind]
        return hop(src.at[r], dst.at[r], far_send.at[kind, c], far_recv.at[kind, c], 6)

    pair_goes_on = jnp.logical_and(is_pair, row < last_row)

    def first_sweep(c):
        r = chunk_rows(c)

        @pl.when(pos != 1)
        def _():
            level_hop(0, c, first_v).wait_recv()
            u = level_in[0, r, :]
            first_v[r, :] = u + (4.0 * h) * act(u, 0) + forcing[r, :]

        @pl.when(jnp.logical_not(is_last))
        def _():
            first_hop(c).start()

        @pl.when(is_a)
        def _():
            mid_hop(0, c, first_v).start()

        @pl.when(pair_goes_on)
        def _():
            below_hop(c).start()

    each(chunks, first_sweep)
    relay_weights(5, PIECES)

    @pl.when(is_pair)
    def _():
        each(chunks, lambda c: far_hop(0, c).wait_recv())
        u = v_in[...]
        own_step[...] = u + (16.0 * h) * act(u, 0)

    is_fourth = me == 3

    @pl.when(is_fourth)
    def _():
        u = inputs[...]
        below_step[...] = u + (16.0 * h) * act(u, 0)

    @pl.when(is_first)
    def _():
        level_in[1] = inputs[...]

    def solved_hop(c):
        r = chunk_rows(c)
        return hop(solved.at[r], solved_in.at[r], solved_send.at[c], solved_recv.at[c], 8)

    def back_hop(c):
        r = chunk_rows(c)
        return hop(solved_a.at[r], solved_back.at[r], back_send.at[0, c], back_recv.at[c], -4)

    def final_hop(c, src):
        r = chunk_rows(c)
        return hop(src.at[r], final_in.at[r], final_send.at[c], final_recv.at[c], 1)

    def final_a_hop(c):
        r = chunk_rows(c)
        return hop(solved_a.at[r], final_in.at[r], back_send.at[1, c], final_recv.at[c], -3)

    def solve_chunk(c, w_a):
        r = chunk_rows(c)
        solved_a[r, :] = w_a
        back_hop(c).start()
        final_a_hop(c).start()
        force = update[r, :] - own_step[r, :]
        w_b = w_a + (16.0 * h) * act(w_a, 0) + force
        solved[r, :] = w_b

        @pl.when(row < last_row)
        def _():
            solved_hop(c).start()
            final_hop(c, solved).start()

        coarse_out[0, r, :] = w_b - relaxed[r, :]

    pair_first = jnp.logical_and(is_pair, row == 0)

    def second_sweep(c):
        r = chunk_rows(c)

        @pl.when(jnp.logical_not(is_first))
        def _():
            level_hop(1, c, update).wait_recv()

        u = level_in[1, r, :]
        new = u + (4.0 * h) * act(u, 0) + forcing[r, :]
        update[r, :] = new

        @pl.when(jnp.logical_not(is_c))
        def _():
            level_hop(1, c, update).start()

        @pl.when(is_relay)
        def _():
            mid_hop(0, c, first_v).wait_recv()
            far_hop(0, c).start()

        @pl.when(is_fourth)
        def _():
            step_two = below_step[r, :]
            update[r, :] = step_two + (new - step_two)

        @pl.when(is_a)
        def _():
            mid_hop(1, c, update).start()

        @pl.when(pair_first)
        def _():
            far_hop(1, c).wait_recv()
            solve_chunk(c, u_in[r, :])

    each(chunks, second_sweep)

    @pl.when(is_relay)
    def _():
        def forward(c):
            mid_hop(1, c, update).wait_recv()
            far_hop(1, c).start()

        each(chunks, forward)

    @pl.when(is_pair)
    def _():
        each(PIECES, lambda i: weight_far(i).wait_recv())
        bias_hop().wait_recv()

    @pl.when(jnp.logical_and(is_pair, row > 0))
    def _():
        each(chunks, lambda c: below_hop(c).wait_recv())
        u = below_in[...]
        below_step[...] = u + (16.0 * h) * act_pair(u)

        def solve_both(c):
            r = chunk_rows(c)
            far_hop(1, c).wait_recv()
            force = u_in[r, :] - below_step[r, :]
            solved_hop(c).wait_recv()
            u = solved_in[r, :]
            solve_chunk(c, u + (16.0 * h) * act_pair(u) + force)

        each(chunks, solve_both)

    @pl.when(is_first)
    def _():
        final_in[...] = inputs[...]

    def final_sweep(c):
        r = chunk_rows(c)

        @pl.when(jnp.logical_not(is_first))
        def _():
            final_hop(c, final_v).wait_recv()

        u = final_in[r, :]
        t = act(u, 0)
        final_v[r, :] = u + (4.0 * h) * t + forcing[r, :]

        @pl.when(jnp.logical_not(is_c))
        def _():
            final_hop(c, final_v).start()

        state[r, :] = u + h * t

    each(chunks, final_sweep)

    def early_hop():
        return hop(early_send, early_in, early_sem.at[0], early_sem.at[1], 4)

    sends_early = jnp.logical_and(jnp.logical_not(is_c), me < blocks - 4)

    @pl.when(sends_early)
    def _():
        early_send[...] = update[...].astype(BF16)
        early_hop().start()

    def a_hop(side, c):
        r = half_rows(c)
        return zhop(
            a_all.at[zed, r],
            a_all.at[zed, r],
            a_send.at[side, c],
            a_recv.at[side, c],
            right if side == 0 else left,
        )

    def a_came(side, c):
        r = half_rows(c)
        source = left if side == 0 else right
        return zhop(
            a_all.at[source, r],
            a_all.at[source, r],
            a_send.at[side, c],
            a_recv.at[side, c],
            right if side == 0 else left,
        )

    def a_relay(side):
        r = half_rows(side)
        source = left if side == 0 else right
        return zhop(
            a_all.at[source, r],
            a_all.at[source, r],
            a_send.at[2, side],
            a_recv.at[2, side],
            right if side == 0 else left,
        )

    def a_relayed(side):
        r = half_rows(side)
        return zhop(
            a_all.at[across, r],
            a_all.at[across, r],
            a_send.at[2, side],
            a_recv.at[2, side],
            right if side == 0 else left,
        )

    def d_hop(j, c):
        r = half_rows(c)
        to = lax.rem(zed + j, planes)
        return zhop(
            d_send.at[to, r], d_all.at[zed, r], d_ssem.at[j - 1, c], d_rsem.at[j - 1, c], to
        )

    def d_came(j, c):
        r = half_rows(c)
        source = lax.rem(zed + planes - j, planes)
        return zhop(
            d_send.at[zed, r], d_all.at[source, r], d_ssem.at[j - 1, c], d_rsem.at[j - 1, c], source
        )

    cols = grad_out.shape[2]

    def block_half(c):
        r = half_rows(c)

        def layer_step(layer, carry):
            u = state[r, :]
            state[r, :] = u + h * act(u, layer)
            return carry

        lax.fori_loop(1, 3, layer_step, 0)
        u = state[r, :]
        x = u.astype(BF16)
        a_all[zed, r, :] = x
        a_hop(0, c).start()
        a_hop(1, c).start()
        t = act(x, 3)
        new_out[0, r, :] = u + h * t
        delta = (adjoint[0, r, :].astype(F32) * h * (1.0 - t * t)).astype(BF16)
        for j in range(planes):
            d_send[j, r, :] = delta[:, j * cols : (j + 1) * cols]
        d_all[zed, r, :] = d_send[zed, r, :]
        for j in range(1, planes):
            d_hop(j, c).start()

    each(halves, block_half)

    for side in range(2):
        a_came(side, side).wait_recv()
        a_relay(side).start()

    @pl.when(jnp.logical_not(is_c))
    def _():
        @pl.when(me >= 4)
        def _():
            early_hop().wait_recv()

        @pl.when(me < 4)
        def _():
            early_in[...] = inputs[...].astype(BF16)

        below_step[...] = early_in[...].astype(F32) + (16.0 * h) * act(early_in[...], 0)
        step_two = below_step[...]
        coarse_out[0] = step_two + (update[...] - step_two) - relaxed[...]

    @pl.when(is_a)
    def _():
        each(chunks, lambda c: back_hop(c).wait_recv())
        coarse_out[0] = solved_back[...] - relaxed[...]

    for side in range(2):
        a_came(side, 1 - side).wait_recv()
    for j in range(1, planes):
        for c in range(halves):
            d_came(j, c).wait_recv()
    for side in range(2):
        a_relayed(side).wait_recv()
    grad_out[0] = lax.dot_general(
        a_all[...].reshape(planes * rows, a_all.shape[2]),
        d_all[...].reshape(planes * rows, cols),
        (((0,), (0,)), ((), ())),
        preferred_element_type=F32,
    )

    @pl.when(jnp.logical_not(is_last))
    def _():
        def sent(c):
            guess_hop(c).wait_send()
            relaxed_hop(c).wait_send()

        each(halves, sent)

        each(chunks, lambda c: first_hop(c).wait_send())

    @pl.when(jnp.logical_not(is_c))
    def _():
        def sent(c):
            level_hop(1, c, update).wait_send()
            final_hop(c, final_v).wait_send()

        each(chunks, sent)

    @pl.when(sends_early)
    def _():
        early_hop().wait_send()

    @pl.when(is_a)
    def _():
        each(PIECES, lambda i: weight_mid(i).wait_send())
        bias_hop().wait_send()

        def sent(c):
            mid_hop(0, c, first_v).wait_send()
            mid_hop(1, c, update).wait_send()

        each(chunks, sent)

    @pl.when(is_relay)
    def _():
        each(PIECES, lambda i: weight_far(i).wait_send())

        def sent(c):
            far_hop(0, c).wait_send()
            far_hop(1, c).wait_send()

        each(chunks, sent)

    @pl.when(is_pair)
    def _():
        def sent(c):
            back_hop(c).wait_send()
            final_a_hop(c).wait_send()

        each(chunks, sent)

    @pl.when(pair_goes_on)
    def _():
        def sent(c):
            below_hop(c).wait_send()
            solved_hop(c).wait_send()
            final_hop(c, solved).wait_send()

        each(chunks, sent)

    for side in range(2):
        for c in range(halves):
            a_hop(side, c).wait_send()
        a_relay(side).wait_send()
    for j in range(1, planes):
        for c in range(halves):
            d_hop(j, c).wait_send()


def solution(mesh):
    blocks, planes = mesh.shape["layer"], mesh.shape["dp"]

    def body(inputs, guesses, weights, biases, adjoint):
        rows, width = inputs.shape
        cols = width // planes
        chunks, halves = rows // CHUNK, rows // HALF
        whole = pltpu.VMEM((rows, width), F32)
        dma = pltpu.SemaphoreType.DMA
        vmem = pl.BlockSpec(memory_space=pltpu.VMEM)
        return pl.pallas_call(
            functools.partial(kernel, blocks),
            out_shape=(
                jax.ShapeDtypeStruct((1, rows, width), F32),
                jax.ShapeDtypeStruct((1, rows, width), F32),
                jax.ShapeDtypeStruct((1, width, cols), F32),
            ),
            in_specs=[vmem, vmem, pl.BlockSpec(memory_space=pl.ANY), vmem, vmem],
            out_specs=(vmem, vmem, vmem),
            scratch_shapes=[
                pltpu.VMEM((4, width, width), BF16),
                whole,
                whole,
                whole,
                whole,
                whole,
                whole,
                whole,
                pltpu.VMEM((2, rows, width), F32),
                whole,
                whole,
                whole,
                whole,
                whole,
                whole,
                whole,
                whole,
                whole,
                whole,
                whole,
                whole,
                whole,
                pltpu.VMEM((width, width), BF16),
                pltpu.VMEM((width, width), BF16),
                pltpu.VMEM((8, width), F32),
                pltpu.VMEM((8, width), F32),
                pltpu.VMEM((rows, width), BF16),
                pltpu.VMEM((rows, width), BF16),
                pltpu.VMEM((planes, rows, width), BF16),
                pltpu.VMEM((planes, rows, cols), BF16),
                pltpu.VMEM((planes, rows, cols), BF16),
                dma((4,)),
                dma((2, halves)),
                dma((2, halves)),
                dma((2, chunks)),
                dma((2, chunks)),
                dma((chunks,)),
                dma((chunks,)),
                dma((chunks,)),
                dma((chunks,)),
                dma((chunks,)),
                dma((chunks,)),
                dma((2, chunks)),
                dma((chunks,)),
                dma((2, chunks)),
                dma((2, chunks)),
                dma((2, chunks)),
                dma((2, chunks)),
                dma((PIECES,)),
                dma((PIECES,)),
                dma((PIECES,)),
                dma((PIECES,)),
                dma((2,)),
                dma((2,)),
                dma((3, halves)),
                dma((3, halves)),
                dma((planes - 1, halves)),
                dma((planes - 1, halves)),
            ],
            compiler_params=pltpu.CompilerParams(
                collective_id=0, has_side_effects=True, vmem_limit_bytes=60 * 1024 * 1024
            ),
            name="mgrit_cycle",
        )(inputs, guesses, weights, biases, adjoint)

    return jax.shard_map(
        body,
        mesh=mesh,
        in_specs=(
            P("dp", None),
            P("layer", "dp", None),
            P("layer", None, None),
            P("layer", None),
            P("layer", "dp", None),
        ),
        out_specs=(P("layer", "dp", None), P("layer", "dp", None), P("layer", None, "dp")),
        check_vma=False,
    )
```

```python
import functools

import jax
import jax.numpy as jnp
from jax import lax
from jax.experimental import pallas as pl
from jax.experimental.pallas import tpu as pltpu
from jax.sharding import PartitionSpec as P

MESH = pl.DeviceIdType.MESH
F32, BF16 = jnp.float32, jnp.bfloat16
CHUNK = 16
HALF = 64
PIECES = 8
VMEM_MAIN = 57 * 1024 * 1024


def kernel(
    blocks,
    inputs,
    guesses,
    weights,
    biases,
    adjoint,
    new_out,
    coarse_out,
    a_all,
    d_all,
    w_v,
    state,
    guess_in,
    relaxed,
    relaxed_in,
    forcing,
    first_v,
    update,
    level_in,
    below_in,
    below_step,
    own_step,
    solved,
    solved_a,
    solved_in,
    solved_back,
    final_v,
    final_in,
    v_mid,
    v_in,
    u_mid,
    u_in,
    w_mid,
    w_pair,
    b_send,
    b_pair,
    early_send,
    early_in,
    guess_16,
    guess_in_16,
    relaxed_16,
    relaxed_in_16,
    new_v,
    coarse_v,
    a_own,
    d_send,
    out_sem,
    w_sem,
    half_send,
    half_recv,
    level_send,
    level_recv,
    below_send,
    below_recv,
    solved_send,
    solved_recv,
    final_send,
    final_recv,
    back_send,
    back_recv,
    mid_send,
    mid_recv,
    far_send,
    far_recv,
    wmid_send,
    wmid_recv,
    wfar_send,
    wfar_recv,
    b_sem,
    early_sem,
    a_send,
    a_recv,
    d_ssem,
    d_rsem,
):
    rows = inputs.shape[0]
    chunks, halves = rows // CHUNK, rows // HALF
    h = 4.0 / (4 * blocks)
    me, zed = lax.axis_index("layer"), lax.axis_index("dp")
    planes = a_all.shape[0]
    pos = lax.rem(me + 1, 4)
    is_first, is_last = me == 0, me == blocks - 1
    is_c = pos == 0
    seat, row = lax.rem(me, 8), me // 8
    is_a, is_pair, is_relay = seat == 3, seat == 7, seat == 1
    last_row = blocks // 8 - 1

    for layer in range(4):
        pltpu.make_async_copy(weights.at[layer], w_v.at[layer], w_sem.at[layer]).start()

    right, left = lax.rem(zed + 1, planes), lax.rem(zed + planes - 1, planes)
    across = lax.rem(zed + 2, planes)
    barrier = pltpu.get_barrier_semaphore()
    near = (1, 2, 3, 4, 6, 7, 8)
    for step in near + tuple(blocks - step for step in near):
        pl.semaphore_signal(
            barrier, inc=1, device_id=(lax.rem(me + step, blocks), zed), device_id_type=MESH
        )
    for other in (right, left, across):
        pl.semaphore_signal(barrier, inc=1, device_id=(me, other), device_id_type=MESH)
    pl.semaphore_wait(barrier, 2 * len(near) + 3)

    def hop(src, dst, send_sem, recv_sem, by):
        return pltpu.make_async_remote_copy(
            src_ref=src,
            dst_ref=dst,
            send_sem=send_sem,
            recv_sem=recv_sem,
            device_id=(lax.rem(me + by + blocks, blocks), zed),
            device_id_type=MESH,
        )

    def zhop(src, dst, send_sem, recv_sem, to):
        return pltpu.make_async_remote_copy(
            src_ref=src,
            dst_ref=dst,
            send_sem=send_sem,
            recv_sem=recv_sem,
            device_id=(me, to),
            device_id_type=MESH,
        )

    def chunk_rows(c):
        return pl.ds(pl.multiple_of(c * CHUNK, CHUNK), CHUNK)

    def half_rows(c):
        return pl.ds(pl.multiple_of(c * HALF, HALF), HALF)

    def act(x, layer):
        z = jnp.dot(x.astype(BF16), w_v[layer], preferred_element_type=F32)
        return jnp.tanh(z + biases[pl.ds(layer, 1), :])

    def act_pair(x):
        z = jnp.dot(x.astype(BF16), w_pair[...], preferred_element_type=F32)
        return jnp.tanh(z + b_pair[0:1, :])

    def each(count, body):
        def step(c, carry):
            body(c)
            return carry

        lax.fori_loop(0, count, step, 0)

    crosses = lax.rem(me, 2) == 1
    came_over = lax.rem(me, 2) == 0
    sends_wide = jnp.logical_not(crosses)
    sends_narrow = jnp.logical_and(crosses, jnp.logical_not(is_last))
    takes_wide = crosses
    takes_narrow = jnp.logical_and(came_over, jnp.logical_not(is_first))

    def guess_hop(c):
        r = half_rows(c)
        return hop(guesses.at[0, r], guess_in.at[r], half_send.at[0, c], half_recv.at[0, c], 1)

    def guess_hop_16(c):
        r = half_rows(c)
        return hop(guess_16.at[r], guess_in_16.at[r], half_send.at[0, c], half_recv.at[0, c], 1)

    @pl.when(sends_wide)
    def _():
        each(halves, lambda c: guess_hop(c).start())

    @pl.when(sends_narrow)
    def _():
        guess_16[...] = guesses[0].astype(BF16)
        each(halves, lambda c: guess_hop_16(c).start())

    @pl.when(is_first)
    def _():
        guess_in[...] = inputs[...]
        relaxed_in[...] = inputs[...]

    def piece_rows(i):
        depth = weights.shape[1] // PIECES
        return pl.ds(pl.multiple_of(i * depth, depth), depth)

    def weight_mid(i):
        r = piece_rows(i)
        return hop(weights.at[0, r], w_mid.at[r], wmid_send.at[i], wmid_recv.at[i], -2)

    def weight_far(i):
        r = piece_rows(i)
        return hop(w_mid.at[r], w_pair.at[r], wfar_send.at[i], wfar_recv.at[i], 6)

    def bias_hop():
        return hop(b_send, b_pair, b_sem.at[0], b_sem.at[1], 4)

    @pl.when(is_a)
    def _():
        each(PIECES, lambda i: weight_mid(i).start())
        b_send[...] = jnp.broadcast_to(biases[0:1, :], b_send.shape)
        bias_hop().start()

    def relay_weights(start, stop):
        @pl.when(is_relay)
        def _():
            def forward(i):
                weight_mid(start + i).wait_recv()
                weight_far(start + i).start()

            each(stop - start, forward)

    def relaxed_hop(c):
        r = half_rows(c)
        return hop(relaxed.at[r], relaxed_in.at[r], half_send.at[1, c], half_recv.at[1, c], 1)

    def relaxed_hop_16(c):
        r = half_rows(c)
        return hop(
            relaxed_16.at[r], relaxed_in_16.at[r], half_send.at[1, c], half_recv.at[1, c], 1
        )

    is_second = pos == 2
    relaxed_wide = jnp.logical_not(jnp.logical_or(is_second, is_last))

    def relax_half(c):
        r = half_rows(c)

        @pl.when(takes_wide)
        def _():
            guess_hop(c).wait_recv()

        @pl.when(takes_narrow)
        def _():
            guess_hop_16(c).wait_recv()
            guess_in[r, :] = guess_in_16[r, :].astype(F32)

        relaxed[r, :] = guess_in[r, :]

        def layer_step(layer, carry):
            @pl.when(c == 0)
            def _():
                pltpu.make_async_copy(weights.at[layer], w_v.at[layer], w_sem.at[layer]).wait()

            u = relaxed[r, :]
            relaxed[r, :] = u + h * act(u, layer)
            return carry

        lax.fori_loop(0, 4, layer_step, 0)

        @pl.when(is_second)
        def _():
            relaxed_16[r, :] = relaxed[r, :].astype(BF16)
            relaxed_hop_16(c).start()

        @pl.when(relaxed_wide)
        def _():
            relaxed_hop(c).start()

    each(halves, relax_half)
    relay_weights(0, 2)

    def forcing_half(c):
        r = half_rows(c)

        @pl.when(pos == 3)
        def _():
            relaxed_hop_16(c).wait_recv()
            relaxed_in[r, :] = relaxed_in_16[r, :].astype(F32)

        @pl.when(jnp.logical_not(jnp.logical_or(is_first, pos == 3)))
        def _():
            relaxed_hop(c).wait_recv()

        u = relaxed_in[r, :]
        t = act(u, 0)
        coarse = u + (4.0 * h) * t
        first_v[r, :] = coarse
        state[r, :] = u + h * t

        def layer_step(layer, carry):
            u = state[r, :]
            state[r, :] = u + h * act(u, layer)
            return carry

        lax.fori_loop(1, 4, layer_step, 0)
        force = state[r, :] - first_v[r, :]
        forcing[r, :] = force
        first_v[r, :] = first_v[r, :] + force

    each(halves, forcing_half)
    relay_weights(2, 5)

    slot = jnp.where(is_c, 1, 0)

    def level_hop(sweep, c, src):
        r = chunk_rows(c)
        return hop(
            src.at[r], level_in.at[sweep, r], level_send.at[sweep, c], level_recv.at[sweep, c], 1
        )

    def first_hop(c):
        r = chunk_rows(c)
        return hop(
            first_v.at[r], level_in.at[slot, r], level_send.at[0, c], level_recv.at[slot, c], 1
        )

    def below_hop(c):
        r = chunk_rows(c)
        return hop(first_v.at[r], below_in.at[r], below_send.at[c], below_recv.at[c], 8)

    def mid_hop(kind, c, src):
        r = chunk_rows(c)
        dst = (v_mid, u_mid)[kind]
        return hop(src.at[r], dst.at[r], mid_send.at[kind, c], mid_recv.at[kind, c], -2)

    def far_hop(kind, c):
        r = chunk_rows(c)
        src, dst = ((v_mid, v_in), (u_mid, u_in))[kind]
        return hop(src.at[r], dst.at[r], far_send.at[kind, c], far_recv.at[kind, c], 6)

    pair_goes_on = jnp.logical_and(is_pair, row < last_row)

    def first_sweep(c):
        r = chunk_rows(c)

        @pl.when(pos != 1)
        def _():
            level_hop(0, c, first_v).wait_recv()
            u = level_in[0, r, :]
            first_v[r, :] = u + (4.0 * h) * act(u, 0) + forcing[r, :]

        @pl.when(jnp.logical_not(is_last))
        def _():
            first_hop(c).start()

        @pl.when(is_a)
        def _():
            mid_hop(0, c, first_v).start()

        @pl.when(pair_goes_on)
        def _():
            below_hop(c).start()

    each(chunks, first_sweep)
    relay_weights(5, PIECES)

    is_fourth = me == 3

    @pl.when(is_fourth)
    def _():
        u = inputs[...]
        below_step[...] = u + (16.0 * h) * act(u, 0)

    @pl.when(is_first)
    def _():
        level_in[1] = inputs[...]

    def solved_hop(c):
        r = chunk_rows(c)
        return hop(solved.at[r], solved_in.at[r], solved_send.at[c], solved_recv.at[c], 8)

    def back_hop(c):
        r = chunk_rows(c)
        return hop(solved_a.at[r], solved_back.at[r], back_send.at[0, c], back_recv.at[c], -4)

    def final_hop(c, src):
        r = chunk_rows(c)
        return hop(src.at[r], final_in.at[r], final_send.at[c], final_recv.at[c], 1)

    def final_row_hop(c):
        r = chunk_rows(c)
        return hop(solved_in.at[r], final_in.at[r], back_send.at[2, c], final_recv.at[c], -7)

    def final_a_hop(c):
        r = chunk_rows(c)
        return hop(solved_a.at[r], final_in.at[r], back_send.at[1, c], final_recv.at[c], -3)

    def solve_chunk(c, w_a):
        r = chunk_rows(c)
        solved_a[r, :] = w_a
        final_a_hop(c).start()
        force = update[r, :] - own_step[r, :]
        w_b = w_a + (16.0 * h) * act(w_a, 0) + force
        solved[r, :] = w_b

        @pl.when(row < last_row)
        def _():
            solved_hop(c).start()

        coarse_v[r, :] = w_b - relaxed[r, :]

    pair_first = jnp.logical_and(is_pair, row == 0)

    def second_sweep(c):
        r = chunk_rows(c)

        @pl.when(jnp.logical_not(is_first))
        def _():
            level_hop(1, c, update).wait_recv()

        @pl.when(jnp.logical_and(is_pair, lax.rem(c, chunks // halves) == 0))
        def _():
            each(chunks // halves, lambda i: far_hop(0, c + i).wait_recv())
            half = half_rows(c // (chunks // halves))
            v_a = v_in[half, :]
            own_step[half, :] = v_a + (16.0 * h) * act(v_a, 0)

        u = level_in[1, r, :]
        new = u + (4.0 * h) * act(u, 0) + forcing[r, :]
        update[r, :] = new

        @pl.when(jnp.logical_not(is_c))
        def _():
            level_hop(1, c, update).start()

        @pl.when(is_fourth)
        def _():
            step_two = below_step[r, :]
            update[r, :] = step_two + (new - step_two)

        @pl.when(is_a)
        def _():
            mid_hop(1, c, update).start()

        @pl.when(pair_first)
        def _():
            far_hop(1, c).wait_recv()
            solve_chunk(c, u_in[r, :])

    each(chunks, second_sweep)

    @pl.when(is_relay)
    def _():
        def forward_v(c):
            mid_hop(0, c, first_v).wait_recv()
            far_hop(0, c).start()

        def forward_u(c):
            mid_hop(1, c, update).wait_recv()
            far_hop(1, c).start()

        each(chunks, forward_v)
        each(chunks, forward_u)

    @pl.when(is_pair)
    def _():
        each(PIECES, lambda i: weight_far(i).wait_recv())
        bias_hop().wait_recv()

    @pl.when(jnp.logical_and(is_pair, row > 0))
    def _():
        each(chunks, lambda c: below_hop(c).wait_recv())
        u = below_in[...]
        below_step[...] = u + (16.0 * h) * act_pair(u)

        def solve_both(c):
            r = chunk_rows(c)
            far_hop(1, c).wait_recv()
            force = u_in[r, :] - below_step[r, :]
            solved_hop(c).wait_recv()
            final_row_hop(c).start()
            u = solved_in[r, :]
            solve_chunk(c, u + (16.0 * h) * act_pair(u) + force)

        each(chunks, solve_both)

    def coarse_copy():
        return pltpu.make_async_copy(coarse_v, coarse_out.at[0], out_sem.at[0, 0])

    @pl.when(is_pair)
    def _():
        each(chunks, lambda c: back_hop(c).start())
        coarse_copy().start()

    @pl.when(is_first)
    def _():
        final_in[...] = inputs[...]

    def final_sweep(c):
        r = chunk_rows(c)

        @pl.when(jnp.logical_not(is_first))
        def _():
            final_hop(c, final_v).wait_recv()

        u = final_in[r, :]
        t = act(u, 0)
        final_v[r, :] = u + (4.0 * h) * t + forcing[r, :]

        @pl.when(jnp.logical_not(is_c))
        def _():
            final_hop(c, final_v).start()

        state[r, :] = u + h * t

    cols = d_send.shape[2]

    def a_hop(side, c):
        r = half_rows(c)
        return zhop(
            a_own.at[r],
            a_all.at[zed, r],
            a_send.at[side, c],
            a_recv.at[side, c],
            right if side == 0 else left,
        )

    def a_came(side, c):
        r = half_rows(c)
        source = left if side == 0 else right
        return zhop(
            a_own.at[r],
            a_all.at[source, r],
            a_send.at[side, c],
            a_recv.at[side, c],
            right if side == 0 else left,
        )

    def a_relay(side):
        r = half_rows(side)
        source = left if side == 0 else right
        return zhop(
            a_all.at[source, r],
            a_all.at[source, r],
            a_send.at[2, side],
            a_recv.at[2, side],
            right if side == 0 else left,
        )

    def a_relayed(side):
        r = half_rows(side)
        return zhop(
            a_own.at[r],
            a_all.at[across, r],
            a_send.at[2, side],
            a_recv.at[2, side],
            right if side == 0 else left,
        )

    def d_hop(j, c):
        r = half_rows(c)
        to = lax.rem(zed + j, planes)
        return zhop(
            d_send.at[to, r], d_all.at[zed, r], d_ssem.at[j - 1, c], d_rsem.at[j - 1, c], to
        )

    def d_came(j, c):
        r = half_rows(c)
        source = lax.rem(zed + planes - j, planes)
        return zhop(
            d_send.at[zed, r], d_all.at[source, r], d_ssem.at[j - 1, c], d_rsem.at[j - 1, c], source
        )

    def own_copies(c):
        r = half_rows(c)
        return (
            pltpu.make_async_copy(new_v.at[r], new_out.at[0, r], out_sem.at[1, c]),
            pltpu.make_async_copy(a_own.at[r], a_all.at[zed, r], out_sem.at[2, c]),
            pltpu.make_async_copy(d_send.at[zed, r], d_all.at[zed, r], out_sem.at[3, c]),
        )

    def block_half(c):
        r = half_rows(c)

        def layer_step(layer, carry):
            u = state[r, :]
            state[r, :] = u + h * act(u, layer)
            return carry

        lax.fori_loop(1, 3, layer_step, 0)
        u = state[r, :]
        x = u.astype(BF16)
        a_own[r, :] = x
        a_hop(0, c).start()
        a_hop(1, c).start()
        t = act(x, 3)
        delta = (adjoint[0, r, :].astype(F32) * h * (1.0 - t * t)).astype(BF16)
        for j in range(planes):
            d_send[j, r, :] = delta[:, j * cols : (j + 1) * cols]
        for j in range(1, planes):
            d_hop(j, c).start()
        new_v[r, :] = u + h * t
        for copy in own_copies(c):
            copy.start()

    def turn(i, carry):
        block = jnp.where(is_c, lax.rem(i, 2), i // halves)
        half = jnp.where(is_c, i // 2, lax.rem(i, halves))

        @pl.when(block == 0)
        def _():
            each(chunks // halves, lambda c: final_sweep(half * (chunks // halves) + c))

        @pl.when(block == 1)
        def _():
            block_half(half)

        return carry

    lax.fori_loop(0, 2 * halves, turn, 0)

    def early_hop():
        return hop(early_send, early_in, early_sem.at[0], early_sem.at[1], 4)

    sends_early = jnp.logical_and(jnp.logical_not(is_c), me < blocks - 4)

    @pl.when(sends_early)
    def _():
        early_send[...] = update[...].astype(BF16)
        early_hop().start()

    for side in range(2):
        a_came(side, side).wait_recv()
        a_relay(side).start()

    @pl.when(jnp.logical_not(is_c))
    def _():
        @pl.when(me >= 4)
        def _():
            early_hop().wait_recv()

        @pl.when(me < 4)
        def _():
            early_in[...] = inputs[...].astype(BF16)

        below_step[...] = early_in[...].astype(F32) + (16.0 * h) * act(early_in[...], 0)
        step_two = below_step[...]
        coarse_v[...] = step_two + (update[...] - step_two) - relaxed[...]

    @pl.when(is_a)
    def _():
        each(chunks, lambda c: back_hop(c).wait_recv())
        coarse_v[...] = solved_back[...] - relaxed[...]

    @pl.when(jnp.logical_not(is_pair))
    def _():
        coarse_copy().start()

    for side in range(2):
        a_came(side, 1 - side).wait_recv()
    for j in range(1, planes):
        for c in range(halves):
            d_came(j, c).wait_recv()
    for side in range(2):
        a_relayed(side).wait_recv()
    coarse_copy().wait()
    for c in range(halves):
        for copy in own_copies(c):
            copy.wait()

    @pl.when(sends_wide)
    def _():
        each(halves, lambda c: guess_hop(c).wait_send())

    @pl.when(sends_narrow)
    def _():
        each(halves, lambda c: guess_hop_16(c).wait_send())

    @pl.when(is_second)
    def _():
        each(halves, lambda c: relaxed_hop_16(c).wait_send())

    @pl.when(relaxed_wide)
    def _():
        each(halves, lambda c: relaxed_hop(c).wait_send())

    @pl.when(jnp.logical_not(is_last))
    def _():
        each(chunks, lambda c: first_hop(c).wait_send())

    @pl.when(jnp.logical_not(is_c))
    def _():
        def sent(c):
            level_hop(1, c, update).wait_send()
            final_hop(c, final_v).wait_send()

        each(chunks, sent)

    @pl.when(sends_early)
    def _():
        early_hop().wait_send()

    @pl.when(is_a)
    def _():
        each(PIECES, lambda i: weight_mid(i).wait_send())
        bias_hop().wait_send()

        def sent(c):
            mid_hop(0, c, first_v).wait_send()
            mid_hop(1, c, update).wait_send()

        each(chunks, sent)

    @pl.when(is_relay)
    def _():
        each(PIECES, lambda i: weight_far(i).wait_send())

        def sent(c):
            far_hop(0, c).wait_send()
            far_hop(1, c).wait_send()

        each(chunks, sent)

    @pl.when(is_pair)
    def _():
        def sent(c):
            back_hop(c).wait_send()
            final_a_hop(c).wait_send()

        each(chunks, sent)

    @pl.when(jnp.logical_and(is_pair, row > 0))
    def _():
        each(chunks, lambda c: final_row_hop(c).wait_send())

    @pl.when(pair_goes_on)
    def _():
        def sent(c):
            below_hop(c).wait_send()
            solved_hop(c).wait_send()

        each(chunks, sent)

    for side in range(2):
        for c in range(halves):
            a_hop(side, c).wait_send()
        a_relay(side).wait_send()
    for j in range(1, planes):
        for c in range(halves):
            d_hop(j, c).wait_send()


def finish(new, coarse, a_all, d_all, new_out, coarse_out, grad_out):
    new_out[...] = new[...]
    coarse_out[...] = coarse[...]
    planes, rows, depth = a_all.shape
    grad_out[0] = lax.dot_general(
        a_all[...].reshape(planes * rows, depth),
        d_all[...].reshape(planes * rows, d_all.shape[2]),
        (((0,), (0,)), ((), ())),
        preferred_element_type=F32,
    )


def solution(mesh):
    blocks, planes = mesh.shape["layer"], mesh.shape["dp"]

    def body(inputs, guesses, weights, biases, adjoint):
        rows, width = inputs.shape
        cols = width // planes
        chunks, halves = rows // CHUNK, rows // HALF
        whole = pltpu.VMEM((rows, width), F32)
        dma = pltpu.SemaphoreType.DMA
        vmem = pl.BlockSpec(memory_space=pltpu.VMEM)
        anywhere = pl.BlockSpec(memory_space=pl.ANY)
        new, coarse, a_all, d_all = pl.pallas_call(
            functools.partial(kernel, blocks),
            out_shape=(
                jax.ShapeDtypeStruct((1, rows, width), F32),
                jax.ShapeDtypeStruct((1, rows, width), F32),
                jax.ShapeDtypeStruct((planes, rows, width), BF16),
                jax.ShapeDtypeStruct((planes, rows, cols), BF16),
            ),
            in_specs=[vmem, vmem, anywhere, vmem, vmem],
            out_specs=(anywhere,) * 4,
            scratch_shapes=[
                pltpu.VMEM((4, width, width), BF16),
                whole,
                whole,
                whole,
                whole,
                whole,
                whole,
                whole,
                pltpu.VMEM((2, rows, width), F32),
                whole,
                whole,
                whole,
                whole,
                whole,
                whole,
                whole,
                whole,
                whole,
                whole,
                whole,
                whole,
                whole,
                pltpu.VMEM((width, width), BF16),
                pltpu.VMEM((width, width), BF16),
                pltpu.VMEM((8, width), F32),
                pltpu.VMEM((8, width), F32),
                pltpu.VMEM((rows, width), BF16),
                pltpu.VMEM((rows, width), BF16),
                pltpu.VMEM((rows, width), BF16),
                pltpu.VMEM((rows, width), BF16),
                pltpu.VMEM((rows, width), BF16),
                pltpu.VMEM((rows, width), BF16),
                whole,
                whole,
                pltpu.VMEM((rows, width), BF16),
                pltpu.VMEM((planes, rows, cols), BF16),
                dma((4, halves)),
                dma((4,)),
                dma((2, halves)),
                dma((2, halves)),
                dma((2, chunks)),
                dma((2, chunks)),
                dma((chunks,)),
                dma((chunks,)),
                dma((chunks,)),
                dma((chunks,)),
                dma((chunks,)),
                dma((chunks,)),
                dma((3, chunks)),
                dma((chunks,)),
                dma((2, chunks)),
                dma((2, chunks)),
                dma((2, chunks)),
                dma((2, chunks)),
                dma((PIECES,)),
                dma((PIECES,)),
                dma((PIECES,)),
                dma((PIECES,)),
                dma((2,)),
                dma((2,)),
                dma((3, halves)),
                dma((3, halves)),
                dma((planes - 1, halves)),
                dma((planes - 1, halves)),
            ],
            compiler_params=pltpu.CompilerParams(
                collective_id=0, has_side_effects=True, vmem_limit_bytes=VMEM_MAIN
            ),
            name="mgrit_cycle",
        )(inputs, guesses, weights, biases, adjoint)
        parts = 4
        slab = pl.BlockSpec((1, rows // parts, width), lambda i: (0, i, 0))
        return pl.pallas_call(
            finish,
            grid=(parts,),
            out_shape=(
                jax.ShapeDtypeStruct((1, rows, width), F32),
                jax.ShapeDtypeStruct((1, rows, width), F32),
                jax.ShapeDtypeStruct((1, width, cols), F32),
            ),
            in_specs=[
                slab,
                slab,
                pl.BlockSpec((planes, rows, width // parts), lambda i: (0, 0, i)),
                pl.BlockSpec((planes, rows, cols), lambda i: (0, 0, 0)),
            ],
            out_specs=(slab, slab, pl.BlockSpec((1, width // parts, cols), lambda i: (0, i, 0))),
            compiler_params=pltpu.CompilerParams(vmem_limit_bytes=16 * 1024 * 1024),
            name="results",
        )(new, coarse, a_all, d_all)

    return jax.shard_map(
        body,
        mesh=mesh,
        in_specs=(
            P("dp", None),
            P("layer", "dp", None),
            P("layer", None, None),
            P("layer", None),
            P("layer", "dp", None),
        ),
        out_specs=(P("layer", "dp", None), P("layer", "dp", None), P("layer", None, "dp")),
        check_vma=False,
    )
```

```python
import functools

import jax
import jax.numpy as jnp
from jax import lax
from jax.experimental import pallas as pl
from jax.experimental.pallas import tpu as pltpu
from jax.sharding import PartitionSpec as P

MESH = pl.DeviceIdType.MESH
F32, BF16 = jnp.float32, jnp.bfloat16
CHUNK = 16
HALF = 64
PIECES = 8
VMEM_MAIN = 40 * 1024 * 1024


def kernel(
    blocks,
    inputs_h,
    guesses_h,
    weights,
    biases_h,
    adjoint_h,
    new_out,
    coarse_out,
    a_all,
    d_all,
    inputs,
    guesses,
    biases,
    adjoint,
    w_v,
    state,
    guess_in,
    relaxed,
    relaxed_in,
    forcing,
    first_v,
    update,
    level_in,
    below_in,
    below_step,
    own_step,
    solved,
    solved_a,
    solved_in,
    solved_back,
    final_v,
    final_in,
    v_in,
    u_in,
    w_pair,
    b_send,
    b_pair,
    early_send,
    early_in,
    guess_16,
    guess_in_16,
    relaxed_16,
    relaxed_in_16,
    new_v,
    coarse_v,
    a_own,
    d_send,
    out_sem,
    in_sem,
    w_sem,
    half_send,
    half_recv,
    level_send,
    level_recv,
    below_send,
    below_recv,
    solved_send,
    solved_recv,
    final_send,
    final_recv,
    back_send,
    back_recv,
    far_send,
    far_recv,
    wfar_send,
    wfar_recv,
    b_sem,
    early_sem,
    a_send,
    a_recv,
    d_ssem,
    d_rsem,
):
    rows = inputs_h.shape[0]
    chunks, halves = rows // CHUNK, rows // HALF
    h = 4.0 / (4 * blocks)
    me, zed = lax.axis_index("layer"), lax.axis_index("dp")
    planes = a_all.shape[0]
    pos = lax.rem(me + 1, 4)
    is_first, is_last = me == 0, me == blocks - 1
    is_c = pos == 0
    seat, row = lax.rem(me, 8), me // 8
    is_a, is_pair = seat == 3, seat == 7
    last_row = blocks // 8 - 1

    arrivals = [
        pltpu.make_async_copy(src, dst, in_sem.at[i])
        for i, (src, dst) in enumerate(
            ((guesses_h, guesses), (biases_h, biases), (inputs_h, inputs), (adjoint_h, adjoint))
        )
    ]
    def weight_copy(layer):
        return pltpu.make_async_copy(weights.at[layer], w_v.at[layer], w_sem.at[layer])

    for copy in arrivals[:3]:
        copy.start()
    weight_copy(0).start()

    right, left = lax.rem(zed + 1, planes), lax.rem(zed + planes - 1, planes)
    across = lax.rem(zed + 2, planes)
    barrier = pltpu.get_barrier_semaphore()
    near = (1, 3, 4, 7, 8)
    for step in near + tuple(blocks - step for step in near):
        pl.semaphore_signal(
            barrier, inc=1, device_id=(lax.rem(me + step, blocks), zed), device_id_type=MESH
        )
    for other in (right, left, across):
        pl.semaphore_signal(barrier, inc=1, device_id=(me, other), device_id_type=MESH)
    pl.semaphore_wait(barrier, 2 * len(near) + 3)

    def hop(src, dst, send_sem, recv_sem, by):
        return pltpu.make_async_remote_copy(
            src_ref=src,
            dst_ref=dst,
            send_sem=send_sem,
            recv_sem=recv_sem,
            device_id=(lax.rem(me + by + blocks, blocks), zed),
            device_id_type=MESH,
        )

    def zhop(src, dst, send_sem, recv_sem, to):
        return pltpu.make_async_remote_copy(
            src_ref=src,
            dst_ref=dst,
            send_sem=send_sem,
            recv_sem=recv_sem,
            device_id=(me, to),
            device_id_type=MESH,
        )

    def chunk_rows(c):
        return pl.ds(pl.multiple_of(c * CHUNK, CHUNK), CHUNK)

    def half_rows(c):
        return pl.ds(pl.multiple_of(c * HALF, HALF), HALF)

    def act(x, layer):
        z = jnp.dot(x.astype(BF16), w_v[layer], preferred_element_type=F32)
        return jnp.tanh(z + biases[pl.ds(layer, 1), :])

    def act_pair(x):
        z = jnp.dot(x.astype(BF16), w_pair[...], preferred_element_type=F32)
        return jnp.tanh(z + b_pair[0:1, :])

    def each(count, body):
        def step(c, carry):
            body(c)
            return carry

        lax.fori_loop(0, count, step, 0)

    for copy in arrivals[:3]:
        copy.wait()
    weight_copy(1).start()

    crosses = lax.rem(me, 2) == 1
    came_over = lax.rem(me, 2) == 0
    sends_wide = jnp.logical_not(crosses)
    sends_narrow = jnp.logical_and(crosses, jnp.logical_not(is_last))
    takes_wide = crosses
    takes_narrow = jnp.logical_and(came_over, jnp.logical_not(is_first))

    def guess_hop(c):
        r = half_rows(c)
        return hop(guesses.at[0, r], guess_in.at[r], half_send.at[0, c], half_recv.at[0, c], 1)

    def guess_hop_16(c):
        r = half_rows(c)
        return hop(guess_16.at[r], guess_in_16.at[r], half_send.at[0, c], half_recv.at[0, c], 1)

    @pl.when(sends_wide)
    def _():
        each(halves, lambda c: guess_hop(c).start())

    @pl.when(sends_narrow)
    def _():
        guess_16[...] = guesses[0].astype(BF16)
        each(halves, lambda c: guess_hop_16(c).start())

    @pl.when(is_first)
    def _():
        guess_in[...] = inputs[...]
        relaxed_in[...] = inputs[...]

    def piece_rows(i):
        depth = weights.shape[1] // PIECES
        return pl.ds(pl.multiple_of(i * depth, depth), depth)

    def weight_far(i):
        r = piece_rows(i)
        return hop(weights.at[0, r], w_pair.at[r], wfar_send.at[i], wfar_recv.at[i], 4)

    def bias_hop():
        return hop(b_send, b_pair, b_sem.at[0], b_sem.at[1], 4)

    @pl.when(is_a)
    def _():
        each(PIECES, lambda i: weight_far(i).start())
        b_send[...] = jnp.broadcast_to(biases[0:1, :], b_send.shape)
        bias_hop().start()

    def relaxed_hop(c):
        r = half_rows(c)
        return hop(relaxed.at[r], relaxed_in.at[r], half_send.at[1, c], half_recv.at[1, c], 1)

    def relaxed_hop_16(c):
        r = half_rows(c)
        return hop(
            relaxed_16.at[r], relaxed_in_16.at[r], half_send.at[1, c], half_recv.at[1, c], 1
        )

    is_second = pos == 2
    relaxed_wide = jnp.logical_not(jnp.logical_or(is_second, is_last))

    def await_guess(c):
        @pl.when(takes_wide)
        def _():
            guess_hop(c).wait_recv()

        @pl.when(takes_narrow)
        def _():
            guess_hop_16(c).wait_recv()

    each(halves, await_guess)

    @pl.when(takes_narrow)
    def _():
        guess_in[...] = guess_in_16[...].astype(F32)

    relaxed[...] = guess_in[...]

    def relax_layer(layer, carry):
        weight_copy(layer).wait()

        @pl.when(layer < 2)
        def _():
            weight_copy(layer + 2).start()

        u = relaxed[...]
        relaxed[...] = u + h * act(u, layer)
        return carry

    lax.fori_loop(0, 4, relax_layer, 0)
    arrivals[3].start()

    @pl.when(is_second)
    def _():
        relaxed_16[...] = relaxed[...].astype(BF16)
        each(halves, lambda c: relaxed_hop_16(c).start())

    @pl.when(relaxed_wide)
    def _():
        each(halves, lambda c: relaxed_hop(c).start())

    slot = jnp.where(is_c, 1, 0)

    def level_hop(sweep, c, src):
        r = chunk_rows(c)
        return hop(
            src.at[r], level_in.at[sweep, r], level_send.at[sweep, c], level_recv.at[sweep, c], 1
        )

    def first_hop(c):
        r = chunk_rows(c)
        return hop(
            first_v.at[r], level_in.at[slot, r], level_send.at[0, c], level_recv.at[slot, c], 1
        )

    def below_hop(c):
        r = chunk_rows(c)
        return hop(first_v.at[r], below_in.at[r], below_send.at[c], below_recv.at[c], 8)

    def far_hop(kind, c):
        r = chunk_rows(c)
        src, dst = ((first_v, v_in), (update, u_in))[kind]
        return hop(src.at[r], dst.at[r], far_send.at[kind, c], far_recv.at[kind, c], 4)

    def forcing_half(c):
        r = half_rows(c)

        @pl.when(pos == 3)
        def _():
            relaxed_hop_16(c).wait_recv()
            relaxed_in[r, :] = relaxed_in_16[r, :].astype(F32)

        @pl.when(jnp.logical_not(jnp.logical_or(is_first, pos == 3)))
        def _():
            relaxed_hop(c).wait_recv()

        u = relaxed_in[r, :]
        t = act(u, 0)
        coarse = u + (4.0 * h) * t
        first_v[r, :] = coarse
        state[r, :] = u + h * t

        def layer_step(layer, carry):
            u = state[r, :]
            state[r, :] = u + h * act(u, layer)
            return carry

        lax.fori_loop(1, 4, layer_step, 0)
        force = state[r, :] - first_v[r, :]
        forcing[r, :] = force
        first_v[r, :] = first_v[r, :] + force

        @pl.when(pos == 1)
        def _():
            each(chunks // halves, lambda i: first_hop(c * (chunks // halves) + i).start())

    each(halves, forcing_half)

    pair_goes_on = jnp.logical_and(is_pair, row < last_row)

    def first_sweep(c):
        r = chunk_rows(c)

        level_hop(0, c, first_v).wait_recv()
        u = level_in[0, r, :]
        first_v[r, :] = u + (4.0 * h) * act(u, 0) + forcing[r, :]

        @pl.when(jnp.logical_not(is_last))
        def _():
            first_hop(c).start()

        @pl.when(is_a)
        def _():
            far_hop(0, c).start()

        @pl.when(pair_goes_on)
        def _():
            below_hop(c).start()

    @pl.when(pos != 1)
    def _():
        each(chunks, first_sweep)

    is_fourth = me == 3

    @pl.when(is_fourth)
    def _():
        u = inputs[...]
        below_step[...] = u + (16.0 * h) * act(u, 0)

    @pl.when(is_first)
    def _():
        level_in[1] = inputs[...]

    def solved_hop(c):
        r = chunk_rows(c)
        return hop(solved.at[r], solved_in.at[r], solved_send.at[c], solved_recv.at[c], 8)

    def back_hop(c):
        r = chunk_rows(c)
        return hop(solved_a.at[r], solved_back.at[r], back_send.at[0, c], back_recv.at[c], -4)

    def final_hop(c, src):
        r = chunk_rows(c)
        return hop(src.at[r], final_in.at[r], final_send.at[c], final_recv.at[c], 1)

    def final_row_hop(c):
        r = chunk_rows(c)
        return hop(solved_in.at[r], final_in.at[r], back_send.at[2, c], final_recv.at[c], -7)

    def final_a_hop(c):
        r = chunk_rows(c)
        return hop(solved_a.at[r], final_in.at[r], back_send.at[1, c], final_recv.at[c], -3)

    def solve_chunk(c, w_a):
        r = chunk_rows(c)
        solved_a[r, :] = w_a
        final_a_hop(c).start()
        force = update[r, :] - own_step[r, :]
        w_b = w_a + (16.0 * h) * act(w_a, 0) + force
        solved[r, :] = w_b

        @pl.when(row < last_row)
        def _():
            solved_hop(c).start()

        coarse_v[r, :] = w_b - relaxed[r, :]

    pair_first = jnp.logical_and(is_pair, row == 0)

    def second_sweep(c):
        r = chunk_rows(c)

        @pl.when(jnp.logical_not(is_first))
        def _():
            level_hop(1, c, update).wait_recv()

        @pl.when(jnp.logical_and(is_pair, lax.rem(c, chunks // halves) == 0))
        def _():
            each(chunks // halves, lambda i: far_hop(0, c + i).wait_recv())
            half = half_rows(c // (chunks // halves))
            v_a = v_in[half, :]
            own_step[half, :] = v_a + (16.0 * h) * act(v_a, 0)

        u = level_in[1, r, :]
        new = u + (4.0 * h) * act(u, 0) + forcing[r, :]
        update[r, :] = new

        @pl.when(jnp.logical_not(is_c))
        def _():
            level_hop(1, c, update).start()

        @pl.when(is_fourth)
        def _():
            step_two = below_step[r, :]
            update[r, :] = step_two + (new - step_two)

        @pl.when(is_a)
        def _():
            far_hop(1, c).start()

        @pl.when(pair_first)
        def _():
            far_hop(1, c).wait_recv()
            solve_chunk(c, u_in[r, :])

    each(chunks, second_sweep)

    @pl.when(is_pair)
    def _():
        each(PIECES, lambda i: weight_far(i).wait_recv())
        bias_hop().wait_recv()

    @pl.when(jnp.logical_and(is_pair, row > 0))
    def _():
        each(chunks, lambda c: below_hop(c).wait_recv())
        u = below_in[...]
        below_step[...] = u + (16.0 * h) * act_pair(u)

        def solve_both(c):
            r = chunk_rows(c)
            far_hop(1, c).wait_recv()
            force = u_in[r, :] - below_step[r, :]
            solved_hop(c).wait_recv()
            final_row_hop(c).start()
            u = solved_in[r, :]
            solve_chunk(c, u + (16.0 * h) * act_pair(u) + force)

        each(chunks, solve_both)

    def coarse_copy():
        return pltpu.make_async_copy(coarse_v, coarse_out.at[0], out_sem.at[0, 0])

    @pl.when(is_pair)
    def _():
        each(chunks, lambda c: back_hop(c).start())
        coarse_copy().start()

    @pl.when(is_first)
    def _():
        final_in[...] = inputs[...]

    def final_sweep(c):
        r = chunk_rows(c)

        @pl.when(jnp.logical_not(is_first))
        def _():
            final_hop(c, final_v).wait_recv()

        u = final_in[r, :]
        t = act(u, 0)
        final_v[r, :] = u + (4.0 * h) * t + forcing[r, :]

        @pl.when(jnp.logical_not(is_c))
        def _():
            final_hop(c, final_v).start()

        state[r, :] = u + h * t

    cols = d_send.shape[2]

    def a_hop(side, c):
        r = half_rows(c)
        return zhop(
            a_own.at[r],
            a_all.at[zed, r],
            a_send.at[side, c],
            a_recv.at[side, c],
            right if side == 0 else left,
        )

    def a_came(side, c):
        r = half_rows(c)
        source = left if side == 0 else right
        return zhop(
            a_own.at[r],
            a_all.at[source, r],
            a_send.at[side, c],
            a_recv.at[side, c],
            right if side == 0 else left,
        )

    def a_relay(side):
        r = half_rows(side)
        source = left if side == 0 else right
        return zhop(
            a_all.at[source, r],
            a_all.at[source, r],
            a_send.at[2, side],
            a_recv.at[2, side],
            right if side == 0 else left,
        )

    def a_relayed(side):
        r = half_rows(side)
        return zhop(
            a_own.at[r],
            a_all.at[across, r],
            a_send.at[2, side],
            a_recv.at[2, side],
            right if side == 0 else left,
        )

    def d_hop(j, c):
        r = half_rows(c)
        to = lax.rem(zed + j, planes)
        return zhop(
            d_send.at[to, r], d_all.at[zed, r], d_ssem.at[j - 1, c], d_rsem.at[j - 1, c], to
        )

    def d_came(j, c):
        r = half_rows(c)
        source = lax.rem(zed + planes - j, planes)
        return zhop(
            d_send.at[zed, r], d_all.at[source, r], d_ssem.at[j - 1, c], d_rsem.at[j - 1, c], source
        )

    def own_copies(c):
        r = half_rows(c)
        return (
            pltpu.make_async_copy(new_v.at[r], new_out.at[0, r], out_sem.at[1, c]),
            pltpu.make_async_copy(a_own.at[r], a_all.at[zed, r], out_sem.at[2, c]),
            pltpu.make_async_copy(d_send.at[zed, r], d_all.at[zed, r], out_sem.at[3, c]),
        )

    def block_half(c):
        r = half_rows(c)

        def layer_step(layer, carry):
            u = state[r, :]
            state[r, :] = u + h * act(u, layer)
            return carry

        lax.fori_loop(1, 3, layer_step, 0)
        u = state[r, :]
        x = u.astype(BF16)
        a_own[r, :] = x
        a_hop(0, c).start()
        a_hop(1, c).start()
        t = act(x, 3)
        delta = (adjoint[0, r, :].astype(F32) * h * (1.0 - t * t)).astype(BF16)
        for j in range(planes):
            d_send[j, r, :] = delta[:, j * cols : (j + 1) * cols]
        for j in range(1, planes):
            d_hop(j, c).start()
        new_v[r, :] = u + h * t
        for copy in own_copies(c):
            copy.start()

    def turn(i, carry):
        block = jnp.where(is_c, lax.rem(i, 2), i // halves)
        half = jnp.where(is_c, i // 2, lax.rem(i, halves))

        @pl.when(block == 0)
        def _():
            each(chunks // halves, lambda c: final_sweep(half * (chunks // halves) + c))

        @pl.when(block == 1)
        def _():
            block_half(half)

        return carry

    arrivals[3].wait()
    lax.fori_loop(0, 2 * halves, turn, 0)

    def early_hop():
        return hop(early_send, early_in, early_sem.at[0], early_sem.at[1], 4)

    sends_early = jnp.logical_and(jnp.logical_not(is_c), me < blocks - 4)

    @pl.when(sends_early)
    def _():
        early_send[...] = update[...].astype(BF16)
        early_hop().start()

    for side in range(2):
        a_came(side, side).wait_recv()
        a_relay(side).start()

    @pl.when(jnp.logical_not(is_c))
    def _():
        @pl.when(me >= 4)
        def _():
            early_hop().wait_recv()

        @pl.when(me < 4)
        def _():
            early_in[...] = inputs[...].astype(BF16)

        below_step[...] = early_in[...].astype(F32) + (16.0 * h) * act(early_in[...], 0)
        step_two = below_step[...]
        coarse_v[...] = step_two + (update[...] - step_two) - relaxed[...]

    @pl.when(is_a)
    def _():
        each(chunks, lambda c: back_hop(c).wait_recv())
        coarse_v[...] = solved_back[...] - relaxed[...]

    @pl.when(jnp.logical_not(is_pair))
    def _():
        coarse_copy().start()

    for side in range(2):
        a_came(side, 1 - side).wait_recv()
    for j in range(1, planes):
        for c in range(halves):
            d_came(j, c).wait_recv()
    for side in range(2):
        a_relayed(side).wait_recv()
    coarse_copy().wait()
    for c in range(halves):
        for copy in own_copies(c):
            copy.wait()

    @pl.when(sends_wide)
    def _():
        each(halves, lambda c: guess_hop(c).wait_send())

    @pl.when(sends_narrow)
    def _():
        each(halves, lambda c: guess_hop_16(c).wait_send())

    @pl.when(is_second)
    def _():
        each(halves, lambda c: relaxed_hop_16(c).wait_send())

    @pl.when(relaxed_wide)
    def _():
        each(halves, lambda c: relaxed_hop(c).wait_send())

    @pl.when(jnp.logical_not(is_last))
    def _():
        each(chunks, lambda c: first_hop(c).wait_send())

    @pl.when(jnp.logical_not(is_c))
    def _():
        def sent(c):
            level_hop(1, c, update).wait_send()
            final_hop(c, final_v).wait_send()

        each(chunks, sent)

    @pl.when(sends_early)
    def _():
        early_hop().wait_send()

    @pl.when(is_a)
    def _():
        each(PIECES, lambda i: weight_far(i).wait_send())
        bias_hop().wait_send()

        def sent(c):
            far_hop(0, c).wait_send()
            far_hop(1, c).wait_send()

        each(chunks, sent)

    @pl.when(is_pair)
    def _():
        def sent(c):
            back_hop(c).wait_send()
            final_a_hop(c).wait_send()

        each(chunks, sent)

    @pl.when(jnp.logical_and(is_pair, row > 0))
    def _():
        each(chunks, lambda c: final_row_hop(c).wait_send())

    @pl.when(pair_goes_on)
    def _():
        def sent(c):
            below_hop(c).wait_send()
            solved_hop(c).wait_send()

        each(chunks, sent)

    for side in range(2):
        for c in range(halves):
            a_hop(side, c).wait_send()
        a_relay(side).wait_send()
    for j in range(1, planes):
        for c in range(halves):
            d_hop(j, c).wait_send()


def finish(new, coarse, a_all, d_all, new_out, coarse_out, grad_out):
    new_out[...] = new[...]
    coarse_out[...] = coarse[...]
    planes, rows, depth = a_all.shape
    grad_out[0] = lax.dot_general(
        a_all[...].reshape(planes * rows, depth),
        d_all[...].reshape(planes * rows, d_all.shape[2]),
        (((0,), (0,)), ((), ())),
        preferred_element_type=F32,
    )


def solution(mesh):
    blocks, planes = mesh.shape["layer"], mesh.shape["dp"]

    def body(inputs, guesses, weights, biases, adjoint):
        rows, width = inputs.shape
        cols = width // planes
        chunks, halves = rows // CHUNK, rows // HALF
        whole = pltpu.VMEM((rows, width), F32)
        dma = pltpu.SemaphoreType.DMA
        anywhere = pl.BlockSpec(memory_space=pl.ANY)
        held = [
            pltpu.with_memory_space_constraint(x, pltpu.HBM)
            for x in (inputs, guesses, weights, biases, adjoint)
        ]
        new, coarse, a_all, d_all = pl.pallas_call(
            functools.partial(kernel, blocks),
            out_shape=(
                jax.ShapeDtypeStruct((1, rows, width), F32),
                jax.ShapeDtypeStruct((1, rows, width), F32),
                jax.ShapeDtypeStruct((planes, rows, width), BF16),
                jax.ShapeDtypeStruct((planes, rows, cols), BF16),
            ),
            in_specs=[pl.BlockSpec(memory_space=pltpu.HBM)] * 5,
            out_specs=(anywhere,) * 4,
            scratch_shapes=[
                pltpu.VMEM((rows, width), F32),
                pltpu.VMEM((1, rows, width), F32),
                pltpu.VMEM((4, width), F32),
                pltpu.VMEM((1, rows, width), BF16),
                pltpu.VMEM((4, width, width), BF16),
                whole,
                whole,
                whole,
                whole,
                whole,
                whole,
                whole,
                pltpu.VMEM((2, rows, width), F32),
                whole,
                whole,
                whole,
                whole,
                whole,
                whole,
                whole,
                whole,
                whole,
                whole,
                whole,
                pltpu.VMEM((width, width), BF16),
                pltpu.VMEM((8, width), F32),
                pltpu.VMEM((8, width), F32),
                pltpu.VMEM((rows, width), BF16),
                pltpu.VMEM((rows, width), BF16),
                pltpu.VMEM((rows, width), BF16),
                pltpu.VMEM((rows, width), BF16),
                pltpu.VMEM((rows, width), BF16),
                pltpu.VMEM((rows, width), BF16),
                whole,
                whole,
                pltpu.VMEM((rows, width), BF16),
                pltpu.VMEM((planes, rows, cols), BF16),
                dma((4, halves)),
                dma((4,)),
                dma((4,)),
                dma((2, halves)),
                dma((2, halves)),
                dma((2, chunks)),
                dma((2, chunks)),
                dma((chunks,)),
                dma((chunks,)),
                dma((chunks,)),
                dma((chunks,)),
                dma((chunks,)),
                dma((chunks,)),
                dma((3, chunks)),
                dma((chunks,)),
                dma((2, chunks)),
                dma((2, chunks)),
                dma((PIECES,)),
                dma((PIECES,)),
                dma((2,)),
                dma((2,)),
                dma((3, halves)),
                dma((3, halves)),
                dma((planes - 1, halves)),
                dma((planes - 1, halves)),
            ],
            compiler_params=pltpu.CompilerParams(
                collective_id=0, has_side_effects=True, vmem_limit_bytes=VMEM_MAIN
            ),
            name="mgrit_cycle",
        )(*held)
        parts = 4
        slab = pl.BlockSpec((1, rows // parts, width), lambda i: (0, i, 0))
        return pl.pallas_call(
            finish,
            grid=(parts,),
            out_shape=(
                jax.ShapeDtypeStruct((1, rows, width), F32),
                jax.ShapeDtypeStruct((1, rows, width), F32),
                jax.ShapeDtypeStruct((1, width, cols), F32),
            ),
            in_specs=[
                slab,
                slab,
                pl.BlockSpec((planes, rows, width // parts), lambda i: (0, 0, i)),
                pl.BlockSpec((planes, rows, cols), lambda i: (0, 0, 0)),
            ],
            out_specs=(slab, slab, pl.BlockSpec((1, width // parts, cols), lambda i: (0, i, 0))),
            compiler_params=pltpu.CompilerParams(vmem_limit_bytes=16 * 1024 * 1024),
            name="results",
        )(new, coarse, a_all, d_all)

    return jax.shard_map(
        body,
        mesh=mesh,
        in_specs=(
            P("dp", None),
            P("layer", "dp", None),
            P("layer", None, None),
            P("layer", None),
            P("layer", "dp", None),
        ),
        out_specs=(P("layer", "dp", None), P("layer", "dp", None), P("layer", None, "dp")),
        check_vma=False,
    )
```

```python
import functools

import jax
import jax.numpy as jnp
from jax import lax
from jax.experimental import pallas as pl
from jax.experimental.pallas import tpu as pltpu
from jax.sharding import PartitionSpec as P

MESH = pl.DeviceIdType.MESH
F32, BF16 = jnp.float32, jnp.bfloat16
CHUNK = 16
HALF = 64
PIECES = 8
VMEM_MAIN = 40 * 1024 * 1024


def kernel(
    blocks,
    inputs_h,
    guesses_h,
    weights,
    biases_h,
    adjoint_h,
    new_out,
    coarse_out,
    grad_out,
    inputs,
    guesses,
    biases,
    adjoint,
    w_v,
    state,
    guess_in,
    relaxed,
    relaxed_in,
    forcing,
    first_v,
    update,
    level_in,
    below_in,
    below_step,
    own_step,
    solved,
    solved_a,
    solved_in,
    solved_back,
    final_v,
    final_in,
    v_in,
    u_in,
    w_pair,
    b_send,
    b_pair,
    early_send,
    early_in,
    guess_16,
    guess_in_16,
    relaxed_16,
    relaxed_in_16,
    a_own,
    a_all,
    adjoint_all,
    in_sem,
    w_sem,
    half_send,
    half_recv,
    level_send,
    level_recv,
    below_send,
    below_recv,
    solved_send,
    solved_recv,
    final_send,
    final_recv,
    back_send,
    back_recv,
    far_send,
    far_recv,
    wfar_send,
    wfar_recv,
    b_sem,
    early_sem,
    a_send,
    a_recv,
    adj_send,
    adj_recv,
):
    rows = inputs_h.shape[0]
    chunks, halves = rows // CHUNK, rows // HALF
    h = 4.0 / (4 * blocks)
    me, zed = lax.axis_index("layer"), lax.axis_index("dp")
    planes = a_all.shape[0]
    pos = lax.rem(me + 1, 4)
    is_first, is_last = me == 0, me == blocks - 1
    is_c = pos == 0
    seat, row = lax.rem(me, 8), me // 8
    is_a, is_pair = seat == 3, seat == 7
    last_row = blocks // 8 - 1

    arrivals = [
        pltpu.make_async_copy(src, dst, in_sem.at[i])
        for i, (src, dst) in enumerate(
            ((guesses_h, guesses), (biases_h, biases), (inputs_h, inputs), (adjoint_h, adjoint))
        )
    ]
    def weight_copy(layer):
        return pltpu.make_async_copy(weights.at[layer], w_v.at[layer], w_sem.at[layer])

    for copy in arrivals[:3]:
        copy.start()
    weight_copy(0).start()

    right, left = lax.rem(zed + 1, planes), lax.rem(zed + planes - 1, planes)
    across = lax.rem(zed + 2, planes)
    barrier = pltpu.get_barrier_semaphore()
    near = (1, 3, 4, 8)
    for step in near + tuple(blocks - step for step in near):
        pl.semaphore_signal(
            barrier, inc=1, device_id=(lax.rem(me + step, blocks), zed), device_id_type=MESH
        )
    for other in (right, left, across):
        pl.semaphore_signal(barrier, inc=1, device_id=(me, other), device_id_type=MESH)
    for copy in arrivals[:3]:
        copy.wait()
    for layer in range(1, 4):
        weight_copy(layer).start()
    arrivals[3].start()
    pl.semaphore_wait(barrier, 2 * len(near) + 3)

    def hop(src, dst, send_sem, recv_sem, by):
        return pltpu.make_async_remote_copy(
            src_ref=src,
            dst_ref=dst,
            send_sem=send_sem,
            recv_sem=recv_sem,
            device_id=(lax.rem(me + by + blocks, blocks), zed),
            device_id_type=MESH,
        )

    def zhop(src, dst, send_sem, recv_sem, to):
        return pltpu.make_async_remote_copy(
            src_ref=src,
            dst_ref=dst,
            send_sem=send_sem,
            recv_sem=recv_sem,
            device_id=(me, to),
            device_id_type=MESH,
        )

    def chunk_rows(c):
        return pl.ds(pl.multiple_of(c * CHUNK, CHUNK), CHUNK)

    def half_rows(c):
        return pl.ds(pl.multiple_of(c * HALF, HALF), HALF)

    def act(x, layer):
        z = jnp.dot(x.astype(BF16), w_v[layer], preferred_element_type=F32)
        return jnp.tanh(z + biases[pl.ds(layer, 1), :])

    def act_pair(x):
        z = jnp.dot(x.astype(BF16), w_pair[...], preferred_element_type=F32)
        return jnp.tanh(z + b_pair[0:1, :])

    def each(count, body):
        def step(c, carry):
            body(c)
            return carry

        lax.fori_loop(0, count, step, 0)

    crosses = lax.rem(me, 2) == 1
    came_over = lax.rem(me, 2) == 0
    sends_wide = jnp.logical_not(crosses)
    sends_narrow = jnp.logical_and(crosses, jnp.logical_not(is_last))
    takes_wide = crosses
    takes_narrow = jnp.logical_and(came_over, jnp.logical_not(is_first))

    def guess_hop(c):
        r = half_rows(c)
        return hop(guesses.at[0, r], guess_in.at[r], half_send.at[0, c], half_recv.at[0, c], 1)

    def guess_hop_16(c):
        r = half_rows(c)
        return hop(guess_16.at[r], guess_in_16.at[r], half_send.at[0, c], half_recv.at[0, c], 1)

    @pl.when(sends_wide)
    def _():
        each(halves, lambda c: guess_hop(c).start())

    @pl.when(sends_narrow)
    def _():
        guess_16[...] = guesses[0].astype(BF16)
        each(halves, lambda c: guess_hop_16(c).start())

    @pl.when(is_first)
    def _():
        guess_in[...] = inputs[...]
        relaxed_in[...] = inputs[...]

    def piece_rows(i):
        depth = weights.shape[1] // PIECES
        return pl.ds(pl.multiple_of(i * depth, depth), depth)

    def weight_far(i):
        r = piece_rows(i)
        return hop(weights.at[0, r], w_pair.at[r], wfar_send.at[i], wfar_recv.at[i], 4)

    def bias_hop():
        return hop(b_send, b_pair, b_sem.at[0], b_sem.at[1], 4)

    weight_leaves = jnp.logical_and(is_a, row > 0)
    weight_comes = jnp.logical_and(is_pair, row > 0)

    @pl.when(weight_leaves)
    def _():
        each(PIECES, lambda i: weight_far(i).start())
        b_send[...] = jnp.broadcast_to(biases[0:1, :], b_send.shape)
        bias_hop().start()

    def relaxed_hop(c):
        r = half_rows(c)
        return hop(relaxed.at[r], relaxed_in.at[r], half_send.at[1, c], half_recv.at[1, c], 1)

    def relaxed_hop_16(c):
        r = half_rows(c)
        return hop(
            relaxed_16.at[r], relaxed_in_16.at[r], half_send.at[1, c], half_recv.at[1, c], 1
        )

    is_second = pos == 2
    relaxed_wide = jnp.logical_not(jnp.logical_or(is_second, is_last))

    def await_guess(c):
        @pl.when(takes_wide)
        def _():
            guess_hop(c).wait_recv()

        @pl.when(takes_narrow)
        def _():
            guess_hop_16(c).wait_recv()

    each(halves, await_guess)

    @pl.when(takes_narrow)
    def _():
        guess_in[...] = guess_in_16[...].astype(F32)

    relaxed[...] = guess_in[...]

    def relax_layer(layer, carry):
        weight_copy(layer).wait()
        u = relaxed[...]
        relaxed[...] = u + h * act(u, layer)
        return carry

    lax.fori_loop(0, 4, relax_layer, 0)

    cols = adjoint_all.shape[2]
    own_cols = pl.ds(pl.multiple_of(zed * cols, cols), cols)

    def adjoint_hop(j):
        to = lax.rem(zed + j, planes)
        to_cols = pl.ds(pl.multiple_of(to * cols, cols), cols)
        return zhop(
            adjoint.at[0, :, to_cols], adjoint_all.at[zed], adj_send.at[j - 1], adj_recv.at[j - 1], to
        )

    def adjoint_came(j):
        source = lax.rem(zed + planes - j, planes)
        return zhop(
            adjoint.at[0, :, own_cols],
            adjoint_all.at[source],
            adj_send.at[j - 1],
            adj_recv.at[j - 1],
            source,
        )

    @pl.when(is_second)
    def _():
        relaxed_16[...] = relaxed[...].astype(BF16)
        each(halves, lambda c: relaxed_hop_16(c).start())

    @pl.when(relaxed_wide)
    def _():
        each(halves, lambda c: relaxed_hop(c).start())

    slot = jnp.where(is_c, 1, 0)

    def level_hop(sweep, c, src):
        r = chunk_rows(c)
        return hop(
            src.at[r], level_in.at[sweep, r], level_send.at[sweep, c], level_recv.at[sweep, c], 1
        )

    def first_hop(c):
        r = chunk_rows(c)
        return hop(
            first_v.at[r], level_in.at[slot, r], level_send.at[0, c], level_recv.at[slot, c], 1
        )

    def below_hop(c):
        r = chunk_rows(c)
        return hop(first_v.at[r], below_in.at[r], below_send.at[c], below_recv.at[c], 8)

    def far_hop(kind, c):
        r = chunk_rows(c)
        src, dst = ((first_v, v_in), (update, u_in))[kind]
        return hop(src.at[r], dst.at[r], far_send.at[kind, c], far_recv.at[kind, c], 4)

    arrivals[3].wait()
    for j in range(1, planes):
        adjoint_hop(j).start()
    adjoint_all[zed] = adjoint[0, :, own_cols]

    def forcing_half(c):
        r = half_rows(c)

        @pl.when(pos == 3)
        def _():
            relaxed_hop_16(c).wait_recv()
            relaxed_in[r, :] = relaxed_in_16[r, :].astype(F32)

        @pl.when(jnp.logical_not(jnp.logical_or(is_first, pos == 3)))
        def _():
            relaxed_hop(c).wait_recv()

        u = relaxed_in[r, :]
        t = act(u, 0)
        coarse = u + (4.0 * h) * t
        first_v[r, :] = coarse
        state[r, :] = u + h * t

        def layer_step(layer, carry):
            u = state[r, :]
            state[r, :] = u + h * act(u, layer)
            return carry

        lax.fori_loop(1, 4, layer_step, 0)
        force = state[r, :] - first_v[r, :]
        forcing[r, :] = force
        first_v[r, :] = first_v[r, :] + force

        @pl.when(pos == 1)
        def _():
            each(chunks // halves, lambda i: first_hop(c * (chunks // halves) + i).start())

    each(halves, forcing_half)

    pair_goes_on = jnp.logical_and(is_pair, row < last_row)

    def first_sweep(c):
        r = chunk_rows(c)

        level_hop(0, c, first_v).wait_recv()
        u = level_in[0, r, :]
        first_v[r, :] = u + (4.0 * h) * act(u, 0) + forcing[r, :]

        @pl.when(jnp.logical_not(is_last))
        def _():
            first_hop(c).start()

        @pl.when(is_a)
        def _():
            far_hop(0, c).start()

        @pl.when(pair_goes_on)
        def _():
            below_hop(c).start()

    @pl.when(pos != 1)
    def _():
        each(chunks, first_sweep)

    is_fourth = me == 3

    @pl.when(is_fourth)
    def _():
        u = inputs[...]
        below_step[...] = u + (16.0 * h) * act(u, 0)

    @pl.when(is_first)
    def _():
        level_in[1] = inputs[...]

    def solved_hop(c):
        r = chunk_rows(c)
        return hop(solved.at[r], solved_in.at[r], solved_send.at[c], solved_recv.at[c], 8)

    def back_hop(c):
        r = chunk_rows(c)
        return hop(solved_a.at[r], solved_back.at[r], back_send.at[0, c], back_recv.at[c], -4)

    def final_hop(c, src):
        r = chunk_rows(c)
        return hop(src.at[r], final_in.at[r], final_send.at[c], final_recv.at[c], 1)

    def final_a_hop(c):
        r = chunk_rows(c)
        return hop(solved_a.at[r], final_in.at[r], back_send.at[1, c], final_recv.at[c], -3)

    def solve_chunk(c, w_a):
        r = chunk_rows(c)
        solved_a[r, :] = w_a
        final_a_hop(c).start()

        @pl.when(row < last_row)
        def _():
            force = update[r, :] - own_step[r, :]
            w_b = w_a + (16.0 * h) * act(w_a, 0) + force
            solved[r, :] = w_b
            solved_hop(c).start()
            final_hop(c, solved).start()
            coarse_out[0, r, :] = w_b - relaxed[r, :]

    pair_first = jnp.logical_and(is_pair, row == 0)

    def second_sweep(c):
        r = chunk_rows(c)

        @pl.when(jnp.logical_not(is_first))
        def _():
            level_hop(1, c, update).wait_recv()

        @pl.when(jnp.logical_and(is_pair, lax.rem(c, chunks // halves) == 0))
        def _():
            each(chunks // halves, lambda i: far_hop(0, c + i).wait_recv())
            half = half_rows(c // (chunks // halves))
            v_a = v_in[half, :]
            own_step[half, :] = v_a + (16.0 * h) * act(v_a, 0)

        u = level_in[1, r, :]
        new = u + (4.0 * h) * act(u, 0) + forcing[r, :]
        update[r, :] = new

        @pl.when(jnp.logical_not(is_c))
        def _():
            level_hop(1, c, update).start()

        @pl.when(is_fourth)
        def _():
            step_two = below_step[r, :]
            update[r, :] = step_two + (new - step_two)

        @pl.when(is_a)
        def _():
            far_hop(1, c).start()

        @pl.when(pair_first)
        def _():
            far_hop(1, c).wait_recv()
            solve_chunk(c, u_in[r, :])

    each(chunks, second_sweep)

    @pl.when(weight_comes)
    def _():
        each(PIECES, lambda i: weight_far(i).wait_recv())
        bias_hop().wait_recv()
        each(chunks, lambda c: below_hop(c).wait_recv())
        u = below_in[...]
        below_step[...] = u + (16.0 * h) * act_pair(u)

        def solve_both(c):
            r = chunk_rows(c)
            far_hop(1, c).wait_recv()
            force = u_in[r, :] - below_step[r, :]
            solved_hop(c).wait_recv()
            u = solved_in[r, :]
            solve_chunk(c, u + (16.0 * h) * act_pair(u) + force)

        each(chunks, solve_both)

    @pl.when(is_last)
    def _():
        w_a = solved_a[...]
        w_b = w_a + (16.0 * h) * act(w_a, 0) + (update[...] - own_step[...])
        coarse_out[0] = w_b - relaxed[...]

    @pl.when(is_pair)
    def _():
        each(chunks, lambda c: back_hop(c).start())

    @pl.when(is_first)
    def _():
        final_in[...] = inputs[...]

    def final_sweep(c):
        r = chunk_rows(c)

        @pl.when(jnp.logical_not(is_first))
        def _():
            final_hop(c, final_v).wait_recv()

        u = final_in[r, :]
        t = act(u, 0)
        final_v[r, :] = u + (4.0 * h) * t + forcing[r, :]

        @pl.when(jnp.logical_not(is_c))
        def _():
            final_hop(c, final_v).start()

        state[r, :] = u + h * t

    def a_hop(side, c):
        r = half_rows(c)
        return zhop(
            a_own.at[r],
            a_all.at[zed, r],
            a_send.at[side, c],
            a_recv.at[side, c],
            right if side == 0 else left,
        )

    def a_came(side, c):
        r = half_rows(c)
        source = left if side == 0 else right
        return zhop(
            a_own.at[r],
            a_all.at[source, r],
            a_send.at[side, c],
            a_recv.at[side, c],
            right if side == 0 else left,
        )

    def a_relay(side):
        r = half_rows(side)
        source = left if side == 0 else right
        return zhop(
            a_all.at[source, r],
            a_all.at[source, r],
            a_send.at[2, side],
            a_recv.at[2, side],
            right if side == 0 else left,
        )

    def a_relayed(side):
        r = half_rows(side)
        return zhop(
            a_own.at[r],
            a_all.at[across, r],
            a_send.at[2, side],
            a_recv.at[2, side],
            right if side == 0 else left,
        )

    def block_half(c):
        r = half_rows(c)

        def layer_step(layer, carry):
            u = state[r, :]
            state[r, :] = u + h * act(u, layer)
            return carry

        lax.fori_loop(1, 3, layer_step, 0)
        u = state[r, :]
        x = u.astype(BF16)
        a_own[r, :] = x
        a_hop(0, c).start()
        a_hop(1, c).start()
        t = act(x, 3)
        new_out[0, r, :] = u + h * t

    def final_half(half):
        each(chunks // halves, lambda c: final_sweep(half * (chunks // halves) + c))
        block_half(half)

    each(halves, final_half)

    def early_hop():
        return hop(early_send, early_in, early_sem.at[0], early_sem.at[1], 4)

    sends_early = jnp.logical_and(jnp.logical_not(is_c), me < blocks - 4)

    @pl.when(sends_early)
    def _():
        early_send[...] = update[...].astype(BF16)
        early_hop().start()

    for side in range(2):
        a_came(side, side).wait_recv()
        a_relay(side).start()

    @pl.when(jnp.logical_not(is_c))
    def _():
        @pl.when(me >= 4)
        def _():
            early_hop().wait_recv()

        @pl.when(me < 4)
        def _():
            early_in[...] = inputs[...].astype(BF16)

        below_step[...] = early_in[...].astype(F32) + (16.0 * h) * act(early_in[...], 0)
        step_two = below_step[...]
        coarse_out[0] = step_two + (update[...] - step_two) - relaxed[...]

    @pl.when(is_a)
    def _():
        each(chunks, lambda c: back_hop(c).wait_recv())
        coarse_out[0] = solved_back[...] - relaxed[...]

    def add_rows(x, source, start):
        z = jnp.dot(x, w_v[3, :, own_cols], preferred_element_type=F32)
        t = jnp.tanh(z + biases[3:4, own_cols])
        delta = (adjoint_all[source].astype(F32) * h * (1.0 - t * t)).astype(BF16)
        part = lax.dot_general(x, delta, (((0,), (0,)), ((), ())), preferred_element_type=F32)
        grad_out[0] = part if start else grad_out[0] + part

    for j in range(1, planes):
        adjoint_came(j).wait_recv()
    add_rows(a_own[...], zed, True)
    for side, source in enumerate((left, right)):
        a_came(side, 1 - side).wait_recv()
        add_rows(a_all[source], source, False)
    for side in range(2):
        a_relayed(side).wait_recv()
    add_rows(a_all[across], across, False)
    @pl.when(sends_wide)
    def _():
        each(halves, lambda c: guess_hop(c).wait_send())

    @pl.when(sends_narrow)
    def _():
        each(halves, lambda c: guess_hop_16(c).wait_send())

    @pl.when(is_second)
    def _():
        each(halves, lambda c: relaxed_hop_16(c).wait_send())

    @pl.when(relaxed_wide)
    def _():
        each(halves, lambda c: relaxed_hop(c).wait_send())

    @pl.when(jnp.logical_not(is_last))
    def _():
        each(chunks, lambda c: first_hop(c).wait_send())

    @pl.when(jnp.logical_not(is_c))
    def _():
        def sent(c):
            level_hop(1, c, update).wait_send()
            final_hop(c, final_v).wait_send()

        each(chunks, sent)

    @pl.when(sends_early)
    def _():
        early_hop().wait_send()

    @pl.when(weight_leaves)
    def _():
        each(PIECES, lambda i: weight_far(i).wait_send())
        bias_hop().wait_send()

    @pl.when(is_a)
    def _():
        def sent(c):
            far_hop(0, c).wait_send()
            far_hop(1, c).wait_send()

        each(chunks, sent)

    @pl.when(is_pair)
    def _():
        def sent(c):
            back_hop(c).wait_send()
            final_a_hop(c).wait_send()

        each(chunks, sent)

    @pl.when(pair_goes_on)
    def _():
        def sent(c):
            below_hop(c).wait_send()
            solved_hop(c).wait_send()
            final_hop(c, solved).wait_send()

        each(chunks, sent)

    for side in range(2):
        for c in range(halves):
            a_hop(side, c).wait_send()
        a_relay(side).wait_send()
    for j in range(1, planes):
        adjoint_hop(j).wait_send()


def finish(*refs):
    copies = [
        pltpu.make_async_copy(src, dst, refs[6].at[i])
        for i, (src, dst) in enumerate(zip(refs[:3], refs[3:6]))
    ]
    for copy in copies:
        copy.start()
    for copy in copies:
        copy.wait()


def solution(mesh):
    blocks, planes = mesh.shape["layer"], mesh.shape["dp"]

    def body(inputs, guesses, weights, biases, adjoint):
        rows, width = inputs.shape
        cols = width // planes
        chunks, halves = rows // CHUNK, rows // HALF
        whole = pltpu.VMEM((rows, width), F32)
        dma = pltpu.SemaphoreType.DMA
        anywhere = pl.BlockSpec(memory_space=pl.ANY)
        held = [
            pltpu.with_memory_space_constraint(x, pltpu.HBM)
            for x in (inputs, guesses, weights, biases, adjoint)
        ]
        results = pl.pallas_call(
            functools.partial(kernel, blocks),
            out_shape=(
                jax.ShapeDtypeStruct((1, rows, width), F32),
                jax.ShapeDtypeStruct((1, rows, width), F32),
                jax.ShapeDtypeStruct((1, width, cols), F32),
            ),
            in_specs=[pl.BlockSpec(memory_space=pltpu.HBM)] * 5,
            out_specs=(pl.BlockSpec(memory_space=pltpu.VMEM),) * 3,
            scratch_shapes=[
                pltpu.VMEM((rows, width), F32),
                pltpu.VMEM((1, rows, width), F32),
                pltpu.VMEM((4, width), F32),
                pltpu.VMEM((1, rows, width), BF16),
                pltpu.VMEM((4, width, width), BF16),
                whole,
                whole,
                whole,
                whole,
                whole,
                whole,
                whole,
                pltpu.VMEM((2, rows, width), F32),
                whole,
                whole,
                whole,
                whole,
                whole,
                whole,
                whole,
                whole,
                whole,
                whole,
                whole,
                pltpu.VMEM((width, width), BF16),
                pltpu.VMEM((8, width), F32),
                pltpu.VMEM((8, width), F32),
                pltpu.VMEM((rows, width), BF16),
                pltpu.VMEM((rows, width), BF16),
                pltpu.VMEM((rows, width), BF16),
                pltpu.VMEM((rows, width), BF16),
                pltpu.VMEM((rows, width), BF16),
                pltpu.VMEM((rows, width), BF16),
                pltpu.VMEM((rows, width), BF16),
                pltpu.VMEM((planes, rows, width), BF16),
                pltpu.VMEM((planes, rows, cols), BF16),
                dma((4,)),
                dma((4,)),
                dma((2, halves)),
                dma((2, halves)),
                dma((2, chunks)),
                dma((2, chunks)),
                dma((chunks,)),
                dma((chunks,)),
                dma((chunks,)),
                dma((chunks,)),
                dma((chunks,)),
                dma((chunks,)),
                dma((2, chunks)),
                dma((chunks,)),
                dma((2, chunks)),
                dma((2, chunks)),
                dma((PIECES,)),
                dma((PIECES,)),
                dma((2,)),
                dma((2,)),
                dma((3, halves)),
                dma((3, halves)),
                dma((planes - 1,)),
                dma((planes - 1,)),
            ],
            compiler_params=pltpu.CompilerParams(
                collective_id=0, has_side_effects=True, vmem_limit_bytes=VMEM_MAIN
            ),
            name="mgrit_cycle",
        )(*held)
        return tuple(
            pl.pallas_call(
                finish,
                out_shape=tuple(jax.ShapeDtypeStruct(x.shape, x.dtype) for x in results),
                in_specs=[pl.BlockSpec(memory_space=pltpu.VMEM)] * 3,
                out_specs=(anywhere,) * 3,
                scratch_shapes=[dma((3,))],
                compiler_params=pltpu.CompilerParams(vmem_limit_bytes=8 * 1024 * 1024),
                name="results",
            )(*results)
        )

    return jax.shard_map(
        body,
        mesh=mesh,
        in_specs=(
            P("dp", None),
            P("layer", "dp", None),
            P("layer", None, None),
            P("layer", None),
            P("layer", "dp", None),
        ),
        out_specs=(P("layer", "dp", None), P("layer", "dp", None), P("layer", None, "dp")),
        check_vma=False,
    )
```

```python
import functools

import jax
import jax.numpy as jnp
from jax import lax
from jax.experimental import pallas as pl
from jax.experimental.pallas import tpu as pltpu
from jax.sharding import PartitionSpec as P

MESH = pl.DeviceIdType.MESH
F32, BF16 = jnp.float32, jnp.bfloat16
CHUNK = 16
HALF = 64
PIECES = 8
VMEM_MAIN = 40 * 1024 * 1024


def kernel(
    blocks,
    inputs_h,
    guesses_h,
    weights,
    biases_h,
    adjoint_h,
    new_out,
    coarse_out,
    grad_out,
    inputs,
    guesses,
    biases,
    adjoint,
    w_v,
    state,
    guess_in,
    relaxed,
    relaxed_in,
    forcing,
    first_v,
    first_16,
    update,
    level_in,
    level_16,
    below_16,
    below_step,
    own_step,
    solved,
    solved_a,
    solved_in,
    solved_back,
    final_v,
    final_in,
    v_in,
    u_in,
    w_pair,
    b_send,
    b_pair,
    early_send,
    early_in,
    guess_16,
    guess_in_16,
    relaxed_16,
    relaxed_in_16,
    a_own,
    a_all,
    adjoint_all,
    in_sem,
    w_sem,
    half_send,
    half_recv,
    level_send,
    level_recv,
    below_send,
    below_recv,
    solved_send,
    solved_recv,
    final_send,
    final_recv,
    back_send,
    back_recv,
    far_send,
    far_recv,
    wfar_send,
    wfar_recv,
    b_sem,
    early_sem,
    a_send,
    a_recv,
    adj_send,
    adj_recv,
):
    rows, width = inputs_h.shape
    chunks, halves = rows // CHUNK, rows // HALF
    h = 4.0 / (4 * blocks)
    me, zed = lax.axis_index("layer"), lax.axis_index("dp")
    planes = a_all.shape[0]
    pos = lax.rem(me + 1, 4)
    is_first, is_last = me == 0, me == blocks - 1
    is_c = pos == 0
    seat, row = lax.rem(me, 8), me // 8
    is_a, is_pair = seat == 3, seat == 7
    last_row = blocks // 8 - 1

    arrivals = [
        pltpu.make_async_copy(src, dst, in_sem.at[i])
        for i, (src, dst) in enumerate(
            ((guesses_h, guesses), (biases_h, biases), (inputs_h, inputs), (adjoint_h, adjoint))
        )
    ]
    def weight_copy(layer):
        return pltpu.make_async_copy(weights.at[layer], w_v.at[layer], w_sem.at[layer])

    for copy in arrivals[:3]:
        copy.start()
    weight_copy(0).start()

    right, left = lax.rem(zed + 1, planes), lax.rem(zed + planes - 1, planes)
    across = lax.rem(zed + 2, planes)
    barrier = pltpu.get_barrier_semaphore()
    near = (1, 3, 4, 8)
    for step in near + tuple(blocks - step for step in near):
        pl.semaphore_signal(
            barrier, inc=1, device_id=(lax.rem(me + step, blocks), zed), device_id_type=MESH
        )
    for other in (right, left, across):
        pl.semaphore_signal(barrier, inc=1, device_id=(me, other), device_id_type=MESH)
    for copy in arrivals[:3]:
        copy.wait()
    for layer in range(1, 4):
        weight_copy(layer).start()
    arrivals[3].start()
    pl.semaphore_wait(barrier, 2 * len(near) + 3)

    def hop(src, dst, send_sem, recv_sem, by):
        return pltpu.make_async_remote_copy(
            src_ref=src,
            dst_ref=dst,
            send_sem=send_sem,
            recv_sem=recv_sem,
            device_id=(lax.rem(me + by + blocks, blocks), zed),
            device_id_type=MESH,
        )

    def zhop(src, dst, send_sem, recv_sem, to):
        return pltpu.make_async_remote_copy(
            src_ref=src,
            dst_ref=dst,
            send_sem=send_sem,
            recv_sem=recv_sem,
            device_id=(me, to),
            device_id_type=MESH,
        )

    def chunk_rows(c):
        return pl.ds(pl.multiple_of(c * CHUNK, CHUNK), CHUNK)

    def half_rows(c):
        return pl.ds(pl.multiple_of(c * HALF, HALF), HALF)

    def act(x, layer):
        z = jnp.dot(x.astype(BF16), w_v[layer], preferred_element_type=F32)
        return jnp.tanh(z + biases[pl.ds(layer, 1), :])

    def act_pair(x):
        z = jnp.dot(x.astype(BF16), w_pair[...], preferred_element_type=F32)
        return jnp.tanh(z + b_pair[0:1, :])

    def each(count, body):
        def step(c, carry):
            body(c)
            return carry

        lax.fori_loop(0, count, step, 0)

    crosses = lax.rem(me, 2) == 1
    came_over = lax.rem(me, 2) == 0
    sends_wide = jnp.logical_not(crosses)
    sends_narrow = jnp.logical_and(crosses, jnp.logical_not(is_last))
    takes_wide = crosses
    takes_narrow = jnp.logical_and(came_over, jnp.logical_not(is_first))

    def guess_hop(c):
        r = half_rows(c)
        return hop(guesses.at[0, r], guess_in.at[r], half_send.at[0, c], half_recv.at[0, c], 1)

    def guess_hop_16(c):
        r = half_rows(c)
        return hop(guess_16.at[r], guess_in_16.at[r], half_send.at[0, c], half_recv.at[0, c], 1)

    @pl.when(sends_wide)
    def _():
        each(halves, lambda c: guess_hop(c).start())

    @pl.when(sends_narrow)
    def _():
        guess_16[...] = guesses[0].astype(BF16)
        each(halves, lambda c: guess_hop_16(c).start())

    @pl.when(is_first)
    def _():
        guess_in[...] = inputs[...]
        relaxed_in[...] = inputs[...]

    def piece_rows(i):
        depth = weights.shape[1] // PIECES
        return pl.ds(pl.multiple_of(i * depth, depth), depth)

    def weight_far(i):
        r = piece_rows(i)
        return hop(weights.at[0, r], w_pair.at[r], wfar_send.at[i], wfar_recv.at[i], 4)

    def bias_hop():
        return hop(b_send, b_pair, b_sem.at[0], b_sem.at[1], 4)

    weight_leaves = jnp.logical_and(is_a, row > 0)
    weight_comes = jnp.logical_and(is_pair, row > 0)

    @pl.when(weight_leaves)
    def _():
        each(PIECES, lambda i: weight_far(i).start())
        b_send[...] = jnp.broadcast_to(biases[0:1, :], b_send.shape)
        bias_hop().start()

    def relaxed_hop(c):
        r = half_rows(c)
        return hop(relaxed.at[r], relaxed_in.at[r], half_send.at[1, c], half_recv.at[1, c], 1)

    def relaxed_hop_16(c):
        r = half_rows(c)
        return hop(
            relaxed_16.at[r], relaxed_in_16.at[r], half_send.at[1, c], half_recv.at[1, c], 1
        )


    def await_guess(c):
        @pl.when(takes_wide)
        def _():
            guess_hop(c).wait_recv()

        @pl.when(takes_narrow)
        def _():
            guess_hop_16(c).wait_recv()

    each(halves, await_guess)

    @pl.when(takes_narrow)
    def _():
        guess_in[...] = guess_in_16[...].astype(F32)

    relaxed[...] = guess_in[...]

    def relax_layer(layer, carry):
        weight_copy(layer).wait()
        u = relaxed[...]
        relaxed[...] = u + h * act(u, layer)
        return carry

    lax.fori_loop(0, 4, relax_layer, 0)

    cols = adjoint_all.shape[2]
    own_cols = pl.ds(pl.multiple_of(zed * cols, cols), cols)

    def adjoint_hop(j):
        to = lax.rem(zed + j, planes)
        to_cols = pl.ds(pl.multiple_of(to * cols, cols), cols)
        return zhop(
            adjoint.at[0, :, to_cols], adjoint_all.at[zed], adj_send.at[j - 1], adj_recv.at[j - 1], to
        )

    def adjoint_came(j):
        source = lax.rem(zed + planes - j, planes)
        return zhop(
            adjoint.at[0, :, own_cols],
            adjoint_all.at[source],
            adj_send.at[j - 1],
            adj_recv.at[j - 1],
            source,
        )

    @pl.when(sends_narrow)
    def _():
        relaxed_16[...] = relaxed[...].astype(BF16)
        each(halves, lambda c: relaxed_hop_16(c).start())

    @pl.when(sends_wide)
    def _():
        each(halves, lambda c: relaxed_hop(c).start())

    slot = jnp.where(is_c, 1, 0)

    def level_hop(sweep, c, src):
        r = chunk_rows(c)
        return hop(
            src.at[r], level_in.at[sweep, r], level_send.at[sweep, c], level_recv.at[sweep, c], 1
        )

    def first_hop(c):
        r = chunk_rows(c)
        return hop(first_v.at[r], level_in.at[0, r], level_send.at[0, c], level_recv.at[0, c], 1)

    def first_hop_16(c):
        r = chunk_rows(c)
        return hop(
            first_16.at[r], level_16.at[slot, r], level_send.at[0, c], level_recv.at[slot, c], 1
        )

    def level_came_16(sweep, c):
        r = chunk_rows(c)
        return hop(
            first_16.at[r],
            level_16.at[sweep, r],
            level_send.at[0, c],
            level_recv.at[sweep, c],
            1,
        )

    def below_hop(c):
        r = chunk_rows(c)
        return hop(first_16.at[r], below_16.at[r], below_send.at[c], below_recv.at[c], 8)

    def far_hop(kind, c):
        r = chunk_rows(c)
        src, dst = ((first_16, v_in), (update, u_in))[kind]
        return hop(src.at[r], dst.at[r], far_send.at[kind, c], far_recv.at[kind, c], 4)

    arrivals[3].wait()
    for j in range(1, planes):
        adjoint_hop(j).start()
    adjoint_all[zed] = adjoint[0, :, own_cols]

    def forcing_half(c):
        r = half_rows(c)

        @pl.when(takes_narrow)
        def _():
            relaxed_hop_16(c).wait_recv()
            relaxed_in[r, :] = relaxed_in_16[r, :].astype(F32)

        @pl.when(takes_wide)
        def _():
            relaxed_hop(c).wait_recv()

        u = relaxed_in[r, :]
        t = act(u, 0)
        coarse = u + (4.0 * h) * t
        first_v[r, :] = coarse
        state[r, :] = u + h * t

        def layer_step(layer, carry):
            u = state[r, :]
            state[r, :] = u + h * act(u, layer)
            return carry

        lax.fori_loop(1, 4, layer_step, 0)
        force = state[r, :] - first_v[r, :]
        forcing[r, :] = force
        first_v[r, :] = first_v[r, :] + force

        @pl.when(pos == 1)
        def _():
            each(chunks // halves, lambda i: first_hop(c * (chunks // halves) + i).start())

    each(halves, forcing_half)

    pair_goes_on = jnp.logical_and(is_pair, row < last_row)

    def first_sweep(c):
        r = chunk_rows(c)

        @pl.when(pos == 3)
        def _():
            level_came_16(0, c).wait_recv()
            level_in[0, r, :] = level_16[0, r, :].astype(F32)

        @pl.when(pos != 3)
        def _():
            level_hop(0, c, first_v).wait_recv()

        u = level_in[0, r, :]
        new = u + (4.0 * h) * act(u, 0) + forcing[r, :]
        narrow = new.astype(BF16)
        first_16[r, :] = narrow
        first_v[r, :] = jnp.where(is_c, narrow.astype(F32), new)

        @pl.when(sends_narrow)
        def _():
            first_hop_16(c).start()

        @pl.when(pos == 3)
        def _():
            first_hop(c).start()

        @pl.when(is_a)
        def _():
            far_hop(0, c).start()

        @pl.when(pair_goes_on)
        def _():
            below_hop(c).start()

    @pl.when(pos != 1)
    def _():
        each(chunks, first_sweep)

    is_fourth = me == 3

    @pl.when(is_fourth)
    def _():
        u = inputs[...]
        below_step[...] = u + (16.0 * h) * act(u, 0)

    @pl.when(is_first)
    def _():
        level_in[1] = inputs[...]

    def solved_hop(c):
        r = chunk_rows(c)
        return hop(solved.at[r], solved_in.at[r], solved_send.at[c], solved_recv.at[c], 8)

    def back_hop(c):
        r = chunk_rows(c)
        return hop(solved_a.at[r], solved_back.at[r], back_send.at[0, c], back_recv.at[c], -4)

    def final_hop(c, src):
        r = chunk_rows(c)
        return hop(src.at[r], final_in.at[r], final_send.at[c], final_recv.at[c], 1)

    def final_a_hop(c):
        r = chunk_rows(c)
        return hop(solved_a.at[r], final_in.at[r], back_send.at[1, c], final_recv.at[c], -3)

    def solve_chunk(c, w_a):
        r = chunk_rows(c)
        solved_a[r, :] = w_a
        final_a_hop(c).start()

        @pl.when(row < last_row)
        def _():
            force = update[r, :] - own_step[r, :]
            w_b = w_a + (16.0 * h) * act(w_a, 0) + force
            solved[r, :] = w_b
            solved_hop(c).start()
            final_hop(c, solved).start()
            coarse_out[0, r, :] = w_b - relaxed[r, :]

    pair_first = jnp.logical_and(is_pair, row == 0)

    def second_sweep(c):
        r = chunk_rows(c)

        @pl.when(jnp.logical_and(pos == 1, jnp.logical_not(is_first)))
        def _():
            level_came_16(1, c).wait_recv()
            level_in[1, r, :] = level_16[1, r, :].astype(F32)

        @pl.when(pos != 1)
        def _():
            level_hop(1, c, update).wait_recv()

        @pl.when(jnp.logical_and(is_pair, lax.rem(c, chunks // halves) == 0))
        def _():
            each(chunks // halves, lambda i: far_hop(0, c + i).wait_recv())
            half = half_rows(c // (chunks // halves))
            v_a = v_in[half, :].astype(F32)
            own_step[half, :] = v_a + (16.0 * h) * act(v_a, 0)

        u = level_in[1, r, :]
        new = u + (4.0 * h) * act(u, 0) + forcing[r, :]
        update[r, :] = new

        @pl.when(jnp.logical_not(is_c))
        def _():
            level_hop(1, c, update).start()

        @pl.when(is_fourth)
        def _():
            step_two = below_step[r, :]
            update[r, :] = step_two + (new - step_two)

        @pl.when(is_a)
        def _():
            far_hop(1, c).start()

        @pl.when(pair_first)
        def _():
            far_hop(1, c).wait_recv()
            solve_chunk(c, u_in[r, :])

    each(chunks, second_sweep)

    @pl.when(weight_comes)
    def _():
        each(PIECES, lambda i: weight_far(i).wait_recv())
        bias_hop().wait_recv()
        each(chunks, lambda c: below_hop(c).wait_recv())
        u = below_16[...].astype(F32)
        below_step[...] = u + (16.0 * h) * act_pair(u)

        def solve_both(c):
            r = chunk_rows(c)
            far_hop(1, c).wait_recv()
            force = u_in[r, :] - below_step[r, :]
            solved_hop(c).wait_recv()
            u = solved_in[r, :]
            solve_chunk(c, u + (16.0 * h) * act_pair(u) + force)

        each(chunks, solve_both)

    @pl.when(is_last)
    def _():
        w_a = solved_a[...]
        w_b = w_a + (16.0 * h) * act(w_a, 0) + (update[...] - own_step[...])
        coarse_out[0] = w_b - relaxed[...]

    @pl.when(is_pair)
    def _():
        each(chunks, lambda c: back_hop(c).start())

    @pl.when(is_first)
    def _():
        final_in[...] = inputs[...]

    def final_sweep(c):
        r = chunk_rows(c)

        @pl.when(jnp.logical_not(is_first))
        def _():
            final_hop(c, final_v).wait_recv()

        u = final_in[r, :]
        t = act(u, 0)
        final_v[r, :] = u + (4.0 * h) * t + forcing[r, :]

        @pl.when(jnp.logical_not(is_c))
        def _():
            final_hop(c, final_v).start()

        state[r, :] = u + h * t

    def a_hop(side, c):
        r = half_rows(c)
        return zhop(
            a_own.at[r],
            a_all.at[zed, r],
            a_send.at[side, c],
            a_recv.at[side, c],
            right if side == 0 else left,
        )

    def a_came(side, c):
        r = half_rows(c)
        source = left if side == 0 else right
        return zhop(
            a_own.at[r],
            a_all.at[source, r],
            a_send.at[side, c],
            a_recv.at[side, c],
            right if side == 0 else left,
        )

    def a_relay(side, c):
        r = half_rows(c)
        part = pl.ds(side * (width // 2), width // 2)
        source = left if side == 0 else right
        return zhop(
            a_all.at[source, r, part],
            a_all.at[source, r, part],
            a_send.at[2 + side, c],
            a_recv.at[2 + side, c],
            right if side == 0 else left,
        )

    def a_relayed(side, c):
        r = half_rows(c)
        part = pl.ds(side * (width // 2), width // 2)
        return zhop(
            a_own.at[r, part],
            a_all.at[across, r, part],
            a_send.at[2 + side, c],
            a_recv.at[2 + side, c],
            right if side == 0 else left,
        )

    def block_half(c):
        r = half_rows(c)

        def layer_step(layer, carry):
            u = state[r, :]
            state[r, :] = u + h * act(u, layer)
            return carry

        lax.fori_loop(1, 3, layer_step, 0)
        u = state[r, :]
        x = u.astype(BF16)
        a_own[r, :] = x
        a_hop(0, c).start()
        a_hop(1, c).start()
        t = act(x, 3)
        new_out[0, r, :] = u + h * t

    def final_half(half):
        each(chunks // halves, lambda c: final_sweep(half * (chunks // halves) + c))
        block_half(half)

    each(halves, final_half)

    def early_hop():
        return hop(early_send, early_in, early_sem.at[0], early_sem.at[1], 4)

    sends_early = jnp.logical_and(jnp.logical_not(is_c), me < blocks - 4)

    @pl.when(sends_early)
    def _():
        early_send[...] = update[...].astype(BF16)
        early_hop().start()

    def add_rows(x, source, start):
        z = jnp.dot(x, w_v[3, :, own_cols], preferred_element_type=F32)
        t = jnp.tanh(z + biases[3:4, own_cols])
        delta = (adjoint_all[source].astype(F32) * h * (1.0 - t * t)).astype(BF16)
        part = lax.dot_general(x, delta, (((0,), (0,)), ((), ())), preferred_element_type=F32)
        grad_out[0] = part if start else grad_out[0] + part

    def pass_on(c):
        for side in range(2):
            a_came(side, c).wait_recv()
            a_relay(side, c).start()

    pass_on(0)
    for j in range(1, planes):
        adjoint_came(j).wait_recv()
    add_rows(a_own[...], zed, True)
    pass_on(1)

    @pl.when(jnp.logical_not(is_c))
    def _():
        @pl.when(me >= 4)
        def _():
            early_hop().wait_recv()

        @pl.when(me < 4)
        def _():
            early_in[...] = inputs[...].astype(BF16)

        below_step[...] = early_in[...].astype(F32) + (16.0 * h) * act(early_in[...], 0)
        step_two = below_step[...]
        coarse_out[0] = step_two + (update[...] - step_two) - relaxed[...]

    @pl.when(is_a)
    def _():
        each(chunks, lambda c: back_hop(c).wait_recv())
        coarse_out[0] = solved_back[...] - relaxed[...]

    add_rows(a_all[left], left, False)
    add_rows(a_all[right], right, False)
    for side in range(2):
        for c in range(halves):
            a_relayed(side, c).wait_recv()
    add_rows(a_all[across], across, False)

    @pl.when(sends_wide)
    def _():
        each(halves, lambda c: guess_hop(c).wait_send())

    @pl.when(sends_narrow)
    def _():
        each(halves, lambda c: guess_hop_16(c).wait_send())

    @pl.when(sends_narrow)
    def _():
        each(halves, lambda c: relaxed_hop_16(c).wait_send())

    @pl.when(sends_wide)
    def _():
        each(halves, lambda c: relaxed_hop(c).wait_send())

    @pl.when(sends_wide)
    def _():
        each(chunks, lambda c: first_hop(c).wait_send())

    @pl.when(sends_narrow)
    def _():
        each(chunks, lambda c: first_hop_16(c).wait_send())

    @pl.when(jnp.logical_not(is_c))
    def _():
        def sent(c):
            level_hop(1, c, update).wait_send()
            final_hop(c, final_v).wait_send()

        each(chunks, sent)

    @pl.when(sends_early)
    def _():
        early_hop().wait_send()

    @pl.when(weight_leaves)
    def _():
        each(PIECES, lambda i: weight_far(i).wait_send())
        bias_hop().wait_send()

    @pl.when(is_a)
    def _():
        def sent(c):
            far_hop(0, c).wait_send()
            far_hop(1, c).wait_send()

        each(chunks, sent)

    @pl.when(is_pair)
    def _():
        def sent(c):
            back_hop(c).wait_send()
            final_a_hop(c).wait_send()

        each(chunks, sent)

    @pl.when(pair_goes_on)
    def _():
        def sent(c):
            below_hop(c).wait_send()
            solved_hop(c).wait_send()
            final_hop(c, solved).wait_send()

        each(chunks, sent)

    for side in range(2):
        for c in range(halves):
            a_hop(side, c).wait_send()
            a_relay(side, c).wait_send()
    for j in range(1, planes):
        adjoint_hop(j).wait_send()


def finish(*refs):
    copies = [
        pltpu.make_async_copy(src, dst, refs[6].at[i])
        for i, (src, dst) in enumerate(zip(refs[:3], refs[3:6]))
    ]
    for copy in copies:
        copy.start()
    for copy in copies:
        copy.wait()


def solution(mesh):
    blocks, planes = mesh.shape["layer"], mesh.shape["dp"]

    def body(inputs, guesses, weights, biases, adjoint):
        rows, width = inputs.shape
        cols = width // planes
        chunks, halves = rows // CHUNK, rows // HALF
        whole = pltpu.VMEM((rows, width), F32)
        dma = pltpu.SemaphoreType.DMA
        anywhere = pl.BlockSpec(memory_space=pl.ANY)
        held = [
            pltpu.with_memory_space_constraint(x, pltpu.HBM)
            for x in (inputs, guesses, weights, biases, adjoint)
        ]
        results = pl.pallas_call(
            functools.partial(kernel, blocks),
            out_shape=(
                jax.ShapeDtypeStruct((1, rows, width), F32),
                jax.ShapeDtypeStruct((1, rows, width), F32),
                jax.ShapeDtypeStruct((1, width, cols), F32),
            ),
            in_specs=[pl.BlockSpec(memory_space=pltpu.HBM)] * 5,
            out_specs=(pl.BlockSpec(memory_space=pltpu.VMEM),) * 3,
            scratch_shapes=[
                pltpu.VMEM((rows, width), F32),
                pltpu.VMEM((1, rows, width), F32),
                pltpu.VMEM((4, width), F32),
                pltpu.VMEM((1, rows, width), BF16),
                pltpu.VMEM((4, width, width), BF16),
                whole,
                whole,
                whole,
                whole,
                whole,
                whole,
                pltpu.VMEM((rows, width), BF16),
                whole,
                pltpu.VMEM((2, rows, width), F32),
                pltpu.VMEM((2, rows, width), BF16),
                pltpu.VMEM((rows, width), BF16),
                whole,
                whole,
                whole,
                whole,
                whole,
                whole,
                whole,
                whole,
                pltpu.VMEM((rows, width), BF16),
                whole,
                pltpu.VMEM((width, width), BF16),
                pltpu.VMEM((8, width), F32),
                pltpu.VMEM((8, width), F32),
                pltpu.VMEM((rows, width), BF16),
                pltpu.VMEM((rows, width), BF16),
                pltpu.VMEM((rows, width), BF16),
                pltpu.VMEM((rows, width), BF16),
                pltpu.VMEM((rows, width), BF16),
                pltpu.VMEM((rows, width), BF16),
                pltpu.VMEM((rows, width), BF16),
                pltpu.VMEM((planes, rows, width), BF16),
                pltpu.VMEM((planes, rows, cols), BF16),
                dma((4,)),
                dma((4,)),
                dma((2, halves)),
                dma((2, halves)),
                dma((2, chunks)),
                dma((2, chunks)),
                dma((chunks,)),
                dma((chunks,)),
                dma((chunks,)),
                dma((chunks,)),
                dma((chunks,)),
                dma((chunks,)),
                dma((2, chunks)),
                dma((chunks,)),
                dma((2, chunks)),
                dma((2, chunks)),
                dma((PIECES,)),
                dma((PIECES,)),
                dma((2,)),
                dma((2,)),
                dma((4, halves)),
                dma((4, halves)),
                dma((planes - 1,)),
                dma((planes - 1,)),
            ],
            compiler_params=pltpu.CompilerParams(
                collective_id=0, has_side_effects=True, vmem_limit_bytes=VMEM_MAIN
            ),
            name="mgrit_cycle",
        )(*held)
        return tuple(
            pl.pallas_call(
                finish,
                out_shape=tuple(jax.ShapeDtypeStruct(x.shape, x.dtype) for x in results),
                in_specs=[pl.BlockSpec(memory_space=pltpu.VMEM)] * 3,
                out_specs=(anywhere,) * 3,
                scratch_shapes=[dma((3,))],
                compiler_params=pltpu.CompilerParams(vmem_limit_bytes=8 * 1024 * 1024),
                name="results",
            )(*results)
        )

    return jax.shard_map(
        body,
        mesh=mesh,
        in_specs=(
            P("dp", None),
            P("layer", "dp", None),
            P("layer", None, None),
            P("layer", None),
            P("layer", "dp", None),
        ),
        out_specs=(P("layer", "dp", None), P("layer", "dp", None), P("layer", None, "dp")),
        check_vma=False,
    )
```

```python
import functools

import jax
import jax.numpy as jnp
from jax import lax
from jax.experimental import pallas as pl
from jax.experimental.pallas import tpu as pltpu
from jax.sharding import PartitionSpec as P

MESH = pl.DeviceIdType.MESH
F32, BF16 = jnp.float32, jnp.bfloat16
CHUNK = 16
HALF = 64
PIECES = 4
VMEM_MAIN = 40 * 1024 * 1024


def kernel(
    blocks,
    inputs_h,
    guesses_h,
    weights,
    biases_h,
    adjoint_h,
    new_out,
    coarse_out,
    grad_out,
    inputs,
    guesses,
    biases,
    adjoint,
    w_v,
    state,
    guess_in,
    relaxed,
    relaxed_in,
    forcing,
    first_v,
    first_16,
    update,
    level_in,
    level_16,
    below_16,
    below_step,
    own_step,
    solved,
    solved_a,
    solved_in,
    solved_back,
    final_v,
    final_in,
    v_in,
    u_in,
    w_pair,
    b_send,
    b_pair,
    early_send,
    early_in,
    guess_16,
    guess_in_16,
    relaxed_16,
    relaxed_in_16,
    a_own,
    a_all,
    adjoint_all,
    in_sem,
    w_sem,
    half_send,
    half_recv,
    level_send,
    level_recv,
    below_send,
    below_recv,
    solved_send,
    solved_recv,
    final_send,
    final_recv,
    back_send,
    back_recv,
    far_send,
    far_recv,
    wfar_send,
    wfar_recv,
    b_sem,
    early_sem,
    a_send,
    a_recv,
    adj_send,
    adj_recv,
):
    rows, width = inputs_h.shape
    chunks, halves = rows // CHUNK, rows // HALF
    h = 4.0 / (4 * blocks)
    me, zed = lax.axis_index("layer"), lax.axis_index("dp")
    planes = a_all.shape[0]
    pos = lax.rem(me + 1, 4)
    is_first, is_last = me == 0, me == blocks - 1
    is_c = pos == 0
    seat, row = lax.rem(me, 8), me // 8
    is_a, is_pair = seat == 3, seat == 7
    last_row = blocks // 8 - 1

    arrivals = [
        pltpu.make_async_copy(src, dst, in_sem.at[i])
        for i, (src, dst) in enumerate(
            ((guesses_h, guesses), (biases_h, biases), (inputs_h, inputs), (adjoint_h, adjoint))
        )
    ]
    def weight_copy(layer):
        return pltpu.make_async_copy(weights.at[layer], w_v.at[layer], w_sem.at[layer])

    for copy in arrivals[:3]:
        copy.start()
    weight_copy(0).start()

    right, left = lax.rem(zed + 1, planes), lax.rem(zed + planes - 1, planes)
    across = lax.rem(zed + 2, planes)
    barrier = pltpu.get_barrier_semaphore()
    near = (1, 3, 4, 8)
    for step in near + tuple(blocks - step for step in near):
        pl.semaphore_signal(
            barrier, inc=1, device_id=(lax.rem(me + step, blocks), zed), device_id_type=MESH
        )
    for other in (right, left, across):
        pl.semaphore_signal(barrier, inc=1, device_id=(me, other), device_id_type=MESH)
    for copy in arrivals[:3]:
        copy.wait()
    for layer in range(1, 4):
        weight_copy(layer).start()
    arrivals[3].start()
    pl.semaphore_wait(barrier, 2 * len(near) + 3)

    def hop(src, dst, send_sem, recv_sem, by):
        return pltpu.make_async_remote_copy(
            src_ref=src,
            dst_ref=dst,
            send_sem=send_sem,
            recv_sem=recv_sem,
            device_id=(lax.rem(me + by + blocks, blocks), zed),
            device_id_type=MESH,
        )

    def zhop(src, dst, send_sem, recv_sem, to):
        return pltpu.make_async_remote_copy(
            src_ref=src,
            dst_ref=dst,
            send_sem=send_sem,
            recv_sem=recv_sem,
            device_id=(me, to),
            device_id_type=MESH,
        )

    def chunk_rows(c):
        return pl.ds(pl.multiple_of(c * CHUNK, CHUNK), CHUNK)

    def half_rows(c):
        return pl.ds(pl.multiple_of(c * HALF, HALF), HALF)

    def act(x, layer):
        z = jnp.dot(x.astype(BF16), w_v[layer], preferred_element_type=F32)
        return jnp.tanh(z + biases[pl.ds(layer, 1), :])

    def act_pair(x):
        z = jnp.dot(x.astype(BF16), w_pair[...], preferred_element_type=F32)
        return jnp.tanh(z + b_pair[0:1, :])

    def each(count, body):
        def step(c, carry):
            body(c)
            return carry

        lax.fori_loop(0, count, step, 0)

    crosses = lax.rem(me, 2) == 1
    came_over = lax.rem(me, 2) == 0
    sends_wide = jnp.logical_not(crosses)
    sends_narrow = jnp.logical_and(crosses, jnp.logical_not(is_last))
    takes_wide = crosses
    takes_narrow = jnp.logical_and(came_over, jnp.logical_not(is_first))

    def guess_hop(c):
        r = half_rows(c)
        return hop(guesses.at[0, r], guess_in.at[r], half_send.at[0, c], half_recv.at[0, c], 1)

    def guess_hop_16(c):
        r = half_rows(c)
        return hop(guess_16.at[r], guess_in_16.at[r], half_send.at[0, c], half_recv.at[0, c], 1)

    @pl.when(sends_wide)
    def _():
        each(halves, lambda c: guess_hop(c).start())

    @pl.when(sends_narrow)
    def _():
        guess_16[...] = guesses[0].astype(BF16)
        each(halves, lambda c: guess_hop_16(c).start())

    @pl.when(is_first)
    def _():
        guess_in[...] = inputs[...]
        relaxed_in[...] = inputs[...]

    def piece_rows(i):
        depth = weights.shape[1] // PIECES
        return pl.ds(pl.multiple_of(i * depth, depth), depth)

    def weight_far(i):
        r = piece_rows(i)
        return hop(weights.at[0, r], w_pair.at[r], wfar_send.at[i], wfar_recv.at[i], 4)

    def bias_hop():
        return hop(b_send, b_pair, b_sem.at[0], b_sem.at[1], 4)

    weight_leaves = jnp.logical_and(is_a, row > 0)
    weight_comes = jnp.logical_and(is_pair, row > 0)

    @pl.when(weight_leaves)
    def _():
        each(PIECES, lambda i: weight_far(i).start())
        b_send[...] = jnp.broadcast_to(biases[0:1, :], b_send.shape)
        bias_hop().start()

    def relaxed_hop(c):
        r = half_rows(c)
        return hop(relaxed.at[r], relaxed_in.at[r], half_send.at[1, c], half_recv.at[1, c], 1)

    def relaxed_hop_16(c):
        r = half_rows(c)
        return hop(
            relaxed_16.at[r], relaxed_in_16.at[r], half_send.at[1, c], half_recv.at[1, c], 1
        )


    def await_guess(c):
        @pl.when(takes_wide)
        def _():
            guess_hop(c).wait_recv()

        @pl.when(takes_narrow)
        def _():
            guess_hop_16(c).wait_recv()

    each(halves, await_guess)

    @pl.when(takes_narrow)
    def _():
        guess_in[...] = guess_in_16[...].astype(F32)

    relaxed[...] = guess_in[...]

    def relax_layer(layer, carry):
        weight_copy(layer).wait()
        u = relaxed[...]
        relaxed[...] = u + h * act(u, layer)
        return carry

    lax.fori_loop(0, 4, relax_layer, 0)

    cols = adjoint_all.shape[2]
    own_cols = pl.ds(pl.multiple_of(zed * cols, cols), cols)

    def adjoint_hop(j):
        to = lax.rem(zed + j, planes)
        to_cols = pl.ds(pl.multiple_of(to * cols, cols), cols)
        return zhop(
            adjoint.at[0, :, to_cols], adjoint_all.at[zed], adj_send.at[j - 1], adj_recv.at[j - 1], to
        )

    def adjoint_came(j):
        source = lax.rem(zed + planes - j, planes)
        return zhop(
            adjoint.at[0, :, own_cols],
            adjoint_all.at[source],
            adj_send.at[j - 1],
            adj_recv.at[j - 1],
            source,
        )

    @pl.when(sends_narrow)
    def _():
        relaxed_16[...] = relaxed[...].astype(BF16)
        each(halves, lambda c: relaxed_hop_16(c).start())

    @pl.when(sends_wide)
    def _():
        each(halves, lambda c: relaxed_hop(c).start())

    slot = jnp.where(is_c, 1, 0)

    def level_hop(sweep, c, src):
        r = chunk_rows(c)
        return hop(
            src.at[r], level_in.at[sweep, r], level_send.at[sweep, c], level_recv.at[sweep, c], 1
        )

    def first_hop(c):
        r = chunk_rows(c)
        return hop(first_v.at[r], level_in.at[0, r], level_send.at[0, c], level_recv.at[0, c], 1)

    def first_hop_16(c):
        r = chunk_rows(c)
        return hop(
            first_16.at[r], level_16.at[slot, r], level_send.at[0, c], level_recv.at[slot, c], 1
        )

    def level_came_16(sweep, c):
        r = chunk_rows(c)
        return hop(
            first_16.at[r],
            level_16.at[sweep, r],
            level_send.at[0, c],
            level_recv.at[sweep, c],
            1,
        )

    def below_hop(c):
        r = chunk_rows(c)
        return hop(first_16.at[r], below_16.at[r], below_send.at[c], below_recv.at[c], 8)

    def far_hop(kind, c):
        r = chunk_rows(c)
        src, dst = ((first_16, v_in), (update, u_in))[kind]
        return hop(src.at[r], dst.at[r], far_send.at[kind, c], far_recv.at[kind, c], 4)

    arrivals[3].wait()
    for j in range(1, planes):
        adjoint_hop(j).start()
    adjoint_all[zed] = adjoint[0, :, own_cols]

    def forcing_half(c):
        r = half_rows(c)

        @pl.when(takes_narrow)
        def _():
            relaxed_hop_16(c).wait_recv()
            relaxed_in[r, :] = relaxed_in_16[r, :].astype(F32)

        @pl.when(takes_wide)
        def _():
            relaxed_hop(c).wait_recv()

        u = relaxed_in[r, :]
        t = act(u, 0)
        coarse = u + (4.0 * h) * t
        first_v[r, :] = coarse
        state[r, :] = u + h * t

        def layer_step(layer, carry):
            u = state[r, :]
            state[r, :] = u + h * act(u, layer)
            return carry

        lax.fori_loop(1, 4, layer_step, 0)
        force = state[r, :] - first_v[r, :]
        forcing[r, :] = force
        first_v[r, :] = first_v[r, :] + force

        @pl.when(pos == 1)
        def _():
            each(chunks // halves, lambda i: first_hop(c * (chunks // halves) + i).start())

    each(halves, forcing_half)

    pair_goes_on = jnp.logical_and(is_pair, row < last_row)

    def first_sweep(c):
        r = chunk_rows(c)

        @pl.when(pos == 3)
        def _():
            level_came_16(0, c).wait_recv()
            level_in[0, r, :] = level_16[0, r, :].astype(F32)

        @pl.when(pos != 3)
        def _():
            level_hop(0, c, first_v).wait_recv()

        u = level_in[0, r, :]
        new = u + (4.0 * h) * act(u, 0) + forcing[r, :]
        narrow = new.astype(BF16)
        first_16[r, :] = narrow
        first_v[r, :] = jnp.where(is_c, narrow.astype(F32), new)

        @pl.when(sends_narrow)
        def _():
            first_hop_16(c).start()

        @pl.when(pos == 3)
        def _():
            first_hop(c).start()

        @pl.when(is_a)
        def _():
            far_hop(0, c).start()

        @pl.when(pair_goes_on)
        def _():
            below_hop(c).start()

    @pl.when(pos != 1)
    def _():
        each(chunks, first_sweep)

    is_fourth = me == 3

    @pl.when(is_fourth)
    def _():
        u = inputs[...]
        below_step[...] = u + (16.0 * h) * act(u, 0)

    @pl.when(is_first)
    def _():
        level_in[1] = inputs[...]

    def solved_hop(c):
        r = chunk_rows(c)
        return hop(solved.at[r], solved_in.at[r], solved_send.at[c], solved_recv.at[c], 8)

    def back_hop(c):
        r = chunk_rows(c)
        return hop(solved_a.at[r], solved_back.at[r], back_send.at[0, c], back_recv.at[c], -4)

    def final_hop(c, src):
        r = chunk_rows(c)
        return hop(src.at[r], final_in.at[r], final_send.at[c], final_recv.at[c], 1)

    def final_a_hop(c):
        r = chunk_rows(c)
        return hop(solved_a.at[r], final_in.at[r], back_send.at[1, c], final_recv.at[c], -3)

    def solve_chunk(c, w_a):
        r = chunk_rows(c)
        solved_a[r, :] = w_a
        final_a_hop(c).start()

        @pl.when(row < last_row)
        def _():
            force = update[r, :] - own_step[r, :]
            w_b = w_a + (16.0 * h) * act(w_a, 0) + force
            solved[r, :] = w_b
            solved_hop(c).start()
            final_hop(c, solved).start()
            coarse_out[0, r, :] = w_b - relaxed[r, :]

    pair_first = jnp.logical_and(is_pair, row == 0)

    def second_sweep(c):
        r = chunk_rows(c)

        @pl.when(jnp.logical_and(pos == 1, jnp.logical_not(is_first)))
        def _():
            level_came_16(1, c).wait_recv()
            level_in[1, r, :] = level_16[1, r, :].astype(F32)

        @pl.when(pos != 1)
        def _():
            level_hop(1, c, update).wait_recv()

        @pl.when(jnp.logical_and(is_pair, lax.rem(c, chunks // halves) == 0))
        def _():
            each(chunks // halves, lambda i: far_hop(0, c + i).wait_recv())
            half = half_rows(c // (chunks // halves))
            v_a = v_in[half, :].astype(F32)
            own_step[half, :] = v_a + (16.0 * h) * act(v_a, 0)

        u = level_in[1, r, :]
        new = u + (4.0 * h) * act(u, 0) + forcing[r, :]
        update[r, :] = new

        @pl.when(jnp.logical_not(is_c))
        def _():
            level_hop(1, c, update).start()

        @pl.when(is_fourth)
        def _():
            step_two = below_step[r, :]
            update[r, :] = step_two + (new - step_two)

        @pl.when(is_a)
        def _():
            far_hop(1, c).start()

        @pl.when(pair_first)
        def _():
            far_hop(1, c).wait_recv()
            solve_chunk(c, u_in[r, :])

    each(chunks, second_sweep)

    @pl.when(weight_comes)
    def _():
        each(PIECES, lambda i: weight_far(i).wait_recv())
        bias_hop().wait_recv()
        each(chunks, lambda c: below_hop(c).wait_recv())
        u = below_16[...].astype(F32)
        below_step[...] = u + (16.0 * h) * act_pair(u)

        def solve_both(c):
            r = chunk_rows(c)
            far_hop(1, c).wait_recv()
            force = u_in[r, :] - below_step[r, :]
            solved_hop(c).wait_recv()
            u = solved_in[r, :]
            solve_chunk(c, u + (16.0 * h) * act_pair(u) + force)

        each(chunks, solve_both)

    @pl.when(is_last)
    def _():
        w_a = solved_a[...]
        w_b = w_a + (16.0 * h) * act(w_a, 0) + (update[...] - own_step[...])
        coarse_out[0] = w_b - relaxed[...]

    @pl.when(is_pair)
    def _():
        each(chunks, lambda c: back_hop(c).start())

    @pl.when(is_first)
    def _():
        final_in[...] = inputs[...]

    def final_sweep(c):
        r = chunk_rows(c)

        @pl.when(jnp.logical_not(is_first))
        def _():
            final_hop(c, final_v).wait_recv()

        u = final_in[r, :]
        t = act(u, 0)
        final_v[r, :] = u + (4.0 * h) * t + forcing[r, :]

        @pl.when(jnp.logical_not(is_c))
        def _():
            final_hop(c, final_v).start()

        state[r, :] = u + h * t

    def a_hop(side, c):
        r = half_rows(c)
        return zhop(
            a_own.at[r],
            a_all.at[zed, r],
            a_send.at[side, c],
            a_recv.at[side, c],
            right if side == 0 else left,
        )

    def a_came(side, c):
        r = half_rows(c)
        source = left if side == 0 else right
        return zhop(
            a_own.at[r],
            a_all.at[source, r],
            a_send.at[side, c],
            a_recv.at[side, c],
            right if side == 0 else left,
        )

    def a_relay(side, c):
        r = half_rows(c)
        part = pl.ds(side * (width // 2), width // 2)
        source = left if side == 0 else right
        return zhop(
            a_all.at[source, r, part],
            a_all.at[source, r, part],
            a_send.at[2 + side, c],
            a_recv.at[2 + side, c],
            right if side == 0 else left,
        )

    def a_relayed(side, c):
        r = half_rows(c)
        part = pl.ds(side * (width // 2), width // 2)
        return zhop(
            a_own.at[r, part],
            a_all.at[across, r, part],
            a_send.at[2 + side, c],
            a_recv.at[2 + side, c],
            right if side == 0 else left,
        )

    def block_half(c):
        r = half_rows(c)

        def layer_step(layer, carry):
            u = state[r, :]
            state[r, :] = u + h * act(u, layer)
            return carry

        lax.fori_loop(1, 3, layer_step, 0)
        u = state[r, :]
        x = u.astype(BF16)
        a_own[r, :] = x
        a_hop(0, c).start()
        a_hop(1, c).start()
        t = act(x, 3)
        new_out[0, r, :] = u + h * t

    mixed = jnp.logical_or(is_c, pos == 3)

    def turn(i):
        block = jnp.where(mixed, lax.rem(i, 2), i // halves)
        half = jnp.where(mixed, i // 2, lax.rem(i, halves))

        @pl.when(block == 0)
        def _():
            each(chunks // halves, lambda c: final_sweep(half * (chunks // halves) + c))

        @pl.when(block == 1)
        def _():
            block_half(half)

    each(2 * halves, turn)

    def early_hop():
        return hop(early_send, early_in, early_sem.at[0], early_sem.at[1], 4)

    sends_early = jnp.logical_and(jnp.logical_not(is_c), me < blocks - 4)

    @pl.when(sends_early)
    def _():
        early_send[...] = update[...].astype(BF16)
        early_hop().start()

    def add_rows(x, source, start):
        z = jnp.dot(x, w_v[3, :, own_cols], preferred_element_type=F32)
        t = jnp.tanh(z + biases[3:4, own_cols])
        delta = (adjoint_all[source].astype(F32) * h * (1.0 - t * t)).astype(BF16)
        part = lax.dot_general(x, delta, (((0,), (0,)), ((), ())), preferred_element_type=F32)
        grad_out[0] = part if start else grad_out[0] + part

    def pass_on(c):
        for side in range(2):
            a_came(side, c).wait_recv()
            a_relay(side, c).start()

    pass_on(0)
    for j in range(1, planes):
        adjoint_came(j).wait_recv()
    add_rows(a_own[...], zed, True)
    pass_on(1)

    @pl.when(jnp.logical_not(is_c))
    def _():
        @pl.when(me >= 4)
        def _():
            early_hop().wait_recv()

        @pl.when(me < 4)
        def _():
            early_in[...] = inputs[...].astype(BF16)

        below_step[...] = early_in[...].astype(F32) + (16.0 * h) * act(early_in[...], 0)
        step_two = below_step[...]
        coarse_out[0] = step_two + (update[...] - step_two) - relaxed[...]

    @pl.when(is_a)
    def _():
        each(chunks, lambda c: back_hop(c).wait_recv())
        coarse_out[0] = solved_back[...] - relaxed[...]

    add_rows(a_all[left], left, False)
    add_rows(a_all[right], right, False)
    for side in range(2):
        for c in range(halves):
            a_relayed(side, c).wait_recv()
    add_rows(a_all[across], across, False)

    @pl.when(sends_wide)
    def _():
        each(halves, lambda c: guess_hop(c).wait_send())

    @pl.when(sends_narrow)
    def _():
        each(halves, lambda c: guess_hop_16(c).wait_send())

    @pl.when(sends_narrow)
    def _():
        each(halves, lambda c: relaxed_hop_16(c).wait_send())

    @pl.when(sends_wide)
    def _():
        each(halves, lambda c: relaxed_hop(c).wait_send())

    @pl.when(sends_wide)
    def _():
        each(chunks, lambda c: first_hop(c).wait_send())

    @pl.when(sends_narrow)
    def _():
        each(chunks, lambda c: first_hop_16(c).wait_send())

    @pl.when(jnp.logical_not(is_c))
    def _():
        def sent(c):
            level_hop(1, c, update).wait_send()
            final_hop(c, final_v).wait_send()

        each(chunks, sent)

    @pl.when(sends_early)
    def _():
        early_hop().wait_send()

    @pl.when(weight_leaves)
    def _():
        each(PIECES, lambda i: weight_far(i).wait_send())
        bias_hop().wait_send()

    @pl.when(is_a)
    def _():
        def sent(c):
            far_hop(0, c).wait_send()
            far_hop(1, c).wait_send()

        each(chunks, sent)

    @pl.when(is_pair)
    def _():
        def sent(c):
            back_hop(c).wait_send()
            final_a_hop(c).wait_send()

        each(chunks, sent)

    @pl.when(pair_goes_on)
    def _():
        def sent(c):
            below_hop(c).wait_send()
            solved_hop(c).wait_send()
            final_hop(c, solved).wait_send()

        each(chunks, sent)

    for side in range(2):
        for c in range(halves):
            a_hop(side, c).wait_send()
            a_relay(side, c).wait_send()
    for j in range(1, planes):
        adjoint_hop(j).wait_send()


def finish(*refs):
    copies = [
        pltpu.make_async_copy(src, dst, refs[6].at[i])
        for i, (src, dst) in enumerate(zip(refs[:3], refs[3:6]))
    ]
    for copy in copies:
        copy.start()
    for copy in copies:
        copy.wait()


def solution(mesh):
    blocks, planes = mesh.shape["layer"], mesh.shape["dp"]

    def body(inputs, guesses, weights, biases, adjoint):
        rows, width = inputs.shape
        cols = width // planes
        chunks, halves = rows // CHUNK, rows // HALF
        whole = pltpu.VMEM((rows, width), F32)
        dma = pltpu.SemaphoreType.DMA
        anywhere = pl.BlockSpec(memory_space=pl.ANY)
        held = [
            pltpu.with_memory_space_constraint(x, pltpu.HBM)
            for x in (inputs, guesses, weights, biases, adjoint)
        ]
        results = pl.pallas_call(
            functools.partial(kernel, blocks),
            out_shape=(
                jax.ShapeDtypeStruct((1, rows, width), F32),
                jax.ShapeDtypeStruct((1, rows, width), F32),
                jax.ShapeDtypeStruct((1, width, cols), F32),
            ),
            in_specs=[pl.BlockSpec(memory_space=pltpu.HBM)] * 5,
            out_specs=(pl.BlockSpec(memory_space=pltpu.VMEM),) * 3,
            scratch_shapes=[
                pltpu.VMEM((rows, width), F32),
                pltpu.VMEM((1, rows, width), F32),
                pltpu.VMEM((4, width), F32),
                pltpu.VMEM((1, rows, width), BF16),
                pltpu.VMEM((4, width, width), BF16),
                whole,
                whole,
                whole,
                whole,
                whole,
                whole,
                pltpu.VMEM((rows, width), BF16),
                whole,
                pltpu.VMEM((2, rows, width), F32),
                pltpu.VMEM((2, rows, width), BF16),
                pltpu.VMEM((rows, width), BF16),
                whole,
                whole,
                whole,
                whole,
                whole,
                whole,
                whole,
                whole,
                pltpu.VMEM((rows, width), BF16),
                whole,
                pltpu.VMEM((width, width), BF16),
                pltpu.VMEM((8, width), F32),
                pltpu.VMEM((8, width), F32),
                pltpu.VMEM((rows, width), BF16),
                pltpu.VMEM((rows, width), BF16),
                pltpu.VMEM((rows, width), BF16),
                pltpu.VMEM((rows, width), BF16),
                pltpu.VMEM((rows, width), BF16),
                pltpu.VMEM((rows, width), BF16),
                pltpu.VMEM((rows, width), BF16),
                pltpu.VMEM((planes, rows, width), BF16),
                pltpu.VMEM((planes, rows, cols), BF16),
                dma((4,)),
                dma((4,)),
                dma((2, halves)),
                dma((2, halves)),
                dma((2, chunks)),
                dma((2, chunks)),
                dma((chunks,)),
                dma((chunks,)),
                dma((chunks,)),
                dma((chunks,)),
                dma((chunks,)),
                dma((chunks,)),
                dma((2, chunks)),
                dma((chunks,)),
                dma((2, chunks)),
                dma((2, chunks)),
                dma((PIECES,)),
                dma((PIECES,)),
                dma((2,)),
                dma((2,)),
                dma((4, halves)),
                dma((4, halves)),
                dma((planes - 1,)),
                dma((planes - 1,)),
            ],
            compiler_params=pltpu.CompilerParams(
                collective_id=0, has_side_effects=True, vmem_limit_bytes=VMEM_MAIN
            ),
            name="mgrit_cycle",
        )(*held)
        return tuple(
            pl.pallas_call(
                finish,
                out_shape=tuple(jax.ShapeDtypeStruct(x.shape, x.dtype) for x in results),
                in_specs=[pl.BlockSpec(memory_space=pltpu.VMEM)] * 3,
                out_specs=(anywhere,) * 3,
                scratch_shapes=[dma((3,))],
                compiler_params=pltpu.CompilerParams(vmem_limit_bytes=8 * 1024 * 1024),
                name="results",
            )(*results)
        )

    return jax.shard_map(
        body,
        mesh=mesh,
        in_specs=(
            P("dp", None),
            P("layer", "dp", None),
            P("layer", None, None),
            P("layer", None),
            P("layer", "dp", None),
        ),
        out_specs=(P("layer", "dp", None), P("layer", "dp", None), P("layer", None, "dp")),
        check_vma=False,
    )
```
